128 devices in a mesh: region: 8 (over x, core), sub: 16 (over y, z).
Axes of the slice: x: 4, y: 4, z: 4, core: 2. Of those that a mesh axis runs over, the one named last changes fastest.
Arguments:
- features: bfloat16 [1024, 128, 256], P(('region', 'sub')), may hold values from -30 to 30
- voxel_mask: int32 [1024, 128], P(('region', 'sub')), may hold values 0 or 1
- counts: int32 [128], replicated, may hold values from 4 to 8, as said below
- neighbors: int32 [1024, 27], P(('region', 'sub')), may hold values from -1 to 1023, as said below
- w_first: bfloat16 [6912, 256], replicated, may hold values from -0.15625 to 0.15625
- w_second: bfloat16 [6912, 256], replicated, may hold values from -0.15625 to 0.15625
- gain_first: float32 [256], replicated, may hold values from 0.1 to 1.9
- bias_first: float32 [256], replicated, may hold values from -3 to 3
- gain_second: float32 [256], replicated, may hold values from 0.1 to 1.9
- bias_second: float32 [256], replicated, may hold values from -3 to 3
- cotangent: bfloat16 [1024, 128, 256], P(('region', 'sub')), may hold values from -30 to 30
Outputs:
- output: bfloat16 [1024, 128, 256], P(('region', 'sub'))
- grad_features: bfloat16 [1024, 128, 256], P(('region', 'sub'))
The draws below stay inside these ranges and needn't reach their ends.
Inputs may be any that keep to these rules, and one draw needn't show every extreme that they name: `counts`: every device has at least one more live brick than 3; some device has 8 and some 3 + 1. `neighbors`: entry 13 of a live slot's row is the slot itself; a slot at or beyond its device's count has -1 in every entry. Slot b names slot c at offset o exactly when c names b at offset 26 - o. Every named slot is live and lies on the same device or on the device just before or just after it in the order of region+sub; a slot on the device after lies among that device's first 3 slots, a slot on the device before among its last 3 live slots.
All inputs are finite; a program needn't handle non-finite values. No bound on the sum of `voxel_mask` on one device may be relied on, other than what follows from the above.
Results may differ from the reference program's by a relative error of at most 0.003.
The reference program's roundings to bfloat16 on the way (of `act_first`, `hidden`, `act_second`, `grad_branch` and `grad_hidden`) count: a program that leaves them out, or rounds other values in their place, can miss the bound.
Values may be sent and summed in bfloat16 or wider, within the bound.
A program may use at most 128 MiB of HBM per device.

```python
import math
import jax
import jax.numpy as jnp
from jax import lax

C = 256
VOX = 128
GC = 8
EDGE = 3
CAP = 8
BRICKS = 1024


def live_layout(key):
    device_total = BRICKS // CAP
    count_key, shuffle_key = jax.random.split(jax.random.fold_in(key, 7))
    live_counts = jax.random.randint(count_key, (device_total,), EDGE + 1, CAP + 1)
    shuffled = jax.random.permutation(shuffle_key, device_total)
    live_counts = live_counts.at[shuffled[0]].set(CAP).at[shuffled[1]].set(EDGE + 1)
    return live_counts.astype(jnp.int32)


def draw_counts(key, part):
    return live_layout(key)


def slot_of(rank_values, starts):
    owner_device = jnp.sum((starts[None, None, :] <= rank_values[:, :, None]).astype(jnp.int32), axis=-1) - 1
    return owner_device * CAP + rank_values - starts[owner_device]


def draw_neighbors(key, part):
    live_counts = live_layout(key)
    reach_key, keep_key = jax.random.split(jax.random.fold_in(key, 11))
    starts = jnp.cumsum(live_counts) - live_counts
    live_total = jnp.sum(live_counts)
    slot_ids = jnp.arange(BRICKS, dtype=jnp.int32)
    owner_device = slot_ids // CAP
    alive_slot = slot_ids % CAP < live_counts[owner_device]
    live_rank = jnp.clip(starts[owner_device] + slot_ids % CAP, 0, BRICKS - 1)
    reach_steps = jax.random.randint(reach_key, (13,), 1, EDGE + 1).at[12].set(EDGE)
    keep_link = (jax.random.randint(keep_key, (BRICKS, 13), 0, 5) < 3).at[:, 12].set(True)
    upper_rank = live_rank[:, None] + reach_steps[None, :]
    lower_rank = live_rank[:, None] - reach_steps[None, :]
    upper_ok = alive_slot[:, None] & (upper_rank < live_total) & keep_link[live_rank]
    lower_keep = jnp.take_along_axis(keep_link, jnp.clip(lower_rank, 0, BRICKS - 1), axis=0)
    lower_ok = alive_slot[:, None] & (lower_rank >= 0) & lower_keep
    upper_ids = jnp.where(upper_ok, slot_of(jnp.clip(upper_rank, 0, live_total - 1), starts), -1)
    lower_ids = jnp.where(lower_ok, slot_of(jnp.clip(lower_rank, 0, live_total - 1), starts), -1)
    center_ids = jnp.where(alive_slot, slot_ids, -1)
    table = jnp.concatenate([lower_ids[:, ::-1], center_ids[:, None], upper_ids], axis=1)
    return table.astype(jnp.int32)


def device_levels(level_key, lowest, highest):
    device_total = BRICKS // CAP
    drawn = jax.random.uniform(level_key, (device_total,), jnp.float32, 0.0, math.log(highest / lowest))
    return jnp.repeat(lowest * jnp.exp(drawn), CAP)


def draw_features(key, part):
    noise_key = jax.random.fold_in(jax.random.fold_in(key, 3), 0)
    group_key = jax.random.fold_in(jax.random.fold_in(key, 3), 2)
    channel_key = jax.random.fold_in(jax.random.fold_in(key, 3), 3)
    level_key = jax.random.fold_in(jax.random.fold_in(key, 3), 4)
    brick_level = device_levels(level_key, 0.6, 4.5)
    group_level = jnp.clip(jax.random.normal(group_key, (C // GC,), jnp.float32), -1.5, 1.5)
    channel_level = 0.3 * jnp.clip(jax.random.normal(channel_key, (C,), jnp.float32), -2.0, 2.0)
    offset = jnp.repeat(group_level, GC) + channel_level
    values = jnp.clip(jax.random.normal(noise_key, (BRICKS, VOX, C), jnp.float32), -4.5, 4.5)
    values = values + offset[None, None, :]
    return (values * brick_level[:, None, None]).astype(jnp.bfloat16)


def draw_cotangent(key, part):
    noise_key, sign_key, group_key, channel_key, level_key = jax.random.split(jax.random.fold_in(key, 5), 5)
    brick_level = device_levels(level_key, 0.3, 3.0)
    group_level = 0.5 + jax.random.uniform(group_key, (C // GC,), jnp.float32, 0.0, 1.0)
    group_sign = jnp.where(jax.random.randint(sign_key, (C // GC,), 0, 2) == 0, -1.0, 1.0)
    channel_level = 0.2 * jnp.clip(jax.random.normal(channel_key, (C,), jnp.float32), -2.0, 2.0)
    offset = jnp.repeat(group_level * group_sign, GC) + channel_level
    values = 0.7 * jnp.clip(jax.random.normal(noise_key, (BRICKS, VOX, C), jnp.float32), -6.0, 6.0)
    values = values + offset[None, None, :]
    return (values * brick_level[:, None, None]).astype(jnp.bfloat16)


def place_ends(values, stream_key, least, high):
    extent = values.shape
    index_at = [jax.random.randint(jax.random.fold_in(stream_key, axis), (), 0, extent[axis]) for axis in range(len(extent))]
    values = values.at[tuple(index_at)].set(least)
    longest = extent.index(max(extent))
    index_at[longest] = (index_at[longest] + 1) % extent[longest]
    return values.at[tuple(index_at)].set(high)


def scatter_about(stream_key, extent, deviation, reach, kind=jnp.bfloat16):
    values = jax.random.normal(stream_key, extent, jnp.float32) * deviation
    return jnp.minimum(jnp.maximum(values, -reach), reach).astype(kind)


def setup_inputs(seed: int = 0) -> dict:
    key_of = jax.random.split(jax.random.key(seed), 12)
    features = draw_features(jax.random.fold_in(key_of[11], 71), 0)
    voxel_mask = place_ends((jax.random.randint(key_of[1], (BRICKS, VOX), 0, 4) < 3).astype(jnp.int32), jax.random.fold_in(key_of[1], 1), 0, 1)
    counts = draw_counts(jax.random.fold_in(key_of[11], 71), 0)
    neighbors = draw_neighbors(jax.random.fold_in(key_of[11], 71), 0)
    w_first = scatter_about(key_of[4], (27 * C, C), (27 * C // 4) ** -0.5, 0.15625)
    w_second = scatter_about(key_of[5], (27 * C, C), (27 * C // 4) ** -0.5, 0.15625)
    gain_first = jnp.clip(1.0 + 0.18 * jax.random.normal(key_of[6], (C,), jnp.float32), 0.1, 1.9)
    bias_first = scatter_about(key_of[7], (C,), 0.5, 3.0, jnp.float32)
    gain_second = jnp.clip(1.0 + 0.18 * jax.random.normal(key_of[8], (C,), jnp.float32), 0.1, 1.9)
    bias_second = scatter_about(key_of[9], (C,), 0.5, 3.0, jnp.float32)
    cotangent = draw_cotangent(jax.random.fold_in(key_of[11], 71), 0)
    return {"features": features, "voxel_mask": voxel_mask, "counts": counts, "neighbors": neighbors, "w_first": w_first, "w_second": w_second, "gain_first": gain_first, "bias_first": bias_first, "gain_second": gain_second, "bias_second": bias_second, "cotangent": cotangent}


eps_norm = 1e-05

def window_columns(brick_grid):
    number = brick_grid.shape[0]
    channels = brick_grid.shape[-1]
    padded_tile = brick_grid.reshape(number, 3, 3, 3, 4, 4, 8, channels)
    padded_tile = padded_tile.transpose(0, 1, 4, 2, 5, 3, 6, 7).reshape(number, 12, 12, 24, channels)
    padded_tile = padded_tile[:, 3:9, 3:9, 7:17]
    windows = [padded_tile[:, offset_x:offset_x + 4, offset_y:offset_y + 4, offset_z:offset_z + 8] for offset_x in range(3) for offset_y in range(3) for offset_z in range(3)]
    return jnp.stack(windows, axis=4).reshape(number * 128, 27 * channels)

def flipped(weights):
    channels = weights.shape[1]
    return weights.reshape(27, channels, channels)[::-1].transpose(0, 2, 1).reshape(27 * channels, channels)

def sparse_conv(activations, neighbors, weights):
    total_slots = activations.shape[0]
    source = jnp.concatenate([activations, jnp.zeros((1,) + activations.shape[1:], activations.dtype)], 0)
    safe_index = jnp.where(neighbors < 0, total_slots, neighbors).astype(jnp.int32)
    blocks = safe_index.reshape(-1, CAP, 27)

    def one_block(block_index):
        brick_grid = source[block_index]
        product = jnp.dot(window_columns(brick_grid), weights, preferred_element_type=jnp.float32)
        return product.reshape(CAP, 128, -1)
    return lax.map(one_block, blocks).reshape(total_slots, 128, -1)

def normalize(values, weight, gain_vec, bias_vec):
    grouped = values.reshape(values.shape[0], values.shape[1], -1, GC)
    group_weight = weight[:, :, None, None]
    voxel_total = jnp.sum(weight) * GC
    group_mean = lax.optimization_barrier(jnp.sum(grouped * group_weight, axis=(0, 1, 3))) / voxel_total
    centered = grouped - group_mean[None, None, :, None]
    spread = lax.optimization_barrier(jnp.sum(centered * centered * group_weight, axis=(0, 1, 3))) / voxel_total
    inv_scale = lax.rsqrt(spread + eps_norm)
    normed = (centered * inv_scale[None, None, :, None]).reshape(values.shape)
    return (normed * gain_vec + bias_vec, normed, inv_scale, voxel_total)

def norm_backward(grad_pre, normed, inv_scale, voxel_total, weight, gain_vec):
    shape_four = (grad_pre.shape[0], grad_pre.shape[1], -1, GC)
    scaled = (grad_pre * gain_vec).reshape(shape_four)
    normed_groups = normed.reshape(shape_four)
    group_weight = weight[:, :, None, None]
    first_sum = lax.optimization_barrier(jnp.sum(scaled * group_weight, axis=(0, 1, 3))) / voxel_total
    second = lax.optimization_barrier(jnp.sum(scaled * normed_groups * group_weight, axis=(0, 1, 3))) / voxel_total
    result = inv_scale[None, None, :, None] * (scaled - first_sum[None, None, :, None] - normed_groups * second[None, None, :, None])
    return result.reshape(grad_pre.shape)

def silu_slope(pre_values):
    sigmoid_part = jax.nn.sigmoid(pre_values)
    return sigmoid_part * (1.0 + pre_values * (1.0 - sigmoid_part))

def reference(features, voxel_mask, counts, neighbors, w_first, w_second, gain_first, bias_first, gain_second, bias_second, cotangent):
    alive_slot = (jnp.arange(CAP)[None, :] < counts[:, None]).reshape(-1)
    weight = voxel_mask.astype(jnp.float32) * alive_slot[:, None].astype(jnp.float32)
    weight_wide = weight[:, :, None]
    inputs = features.astype(jnp.float32) * weight_wide
    pre_first, normed_first, scale_first, voxel_total = normalize(inputs, weight, gain_first, bias_first)
    act_first = (jax.nn.silu(pre_first) * weight_wide).astype(jnp.bfloat16)
    hidden = (sparse_conv(act_first, neighbors, w_first) * weight_wide).astype(jnp.bfloat16)
    pre_second, normed_second, scale_second, voxel_total = normalize(hidden.astype(jnp.float32), weight, gain_second, bias_second)
    act_second = (jax.nn.silu(pre_second) * weight_wide).astype(jnp.bfloat16)
    branch = sparse_conv(act_second, neighbors, w_second)
    output = ((inputs + branch) * weight_wide).astype(jnp.bfloat16)
    grad_branch = (cotangent.astype(jnp.float32) * weight_wide).astype(jnp.bfloat16)
    grad_act_second = sparse_conv(grad_branch, neighbors, flipped(w_second))
    grad_pre_second = grad_act_second * silu_slope(pre_second) * weight_wide
    grad_hidden = (norm_backward(grad_pre_second, normed_second, scale_second, voxel_total, weight, gain_second) * weight_wide).astype(jnp.bfloat16)
    grad_act_first = sparse_conv(grad_hidden, neighbors, flipped(w_first))
    grad_pre_first = grad_act_first * silu_slope(pre_first) * weight_wide
    grad_inputs = norm_backward(grad_pre_first, normed_first, scale_first, voxel_total, weight, gain_first)
    grad_features = ((cotangent.astype(jnp.float32) + grad_inputs) * weight_wide).astype(jnp.bfloat16)
    return (output, grad_features)
```

```python
import functools

import jax
import jax.numpy as jnp
from jax import lax
from jax.experimental import pallas as pl
from jax.experimental.pallas import tpu as pltpu
from jax.sharding import PartitionSpec as P

GC = 8
CAP = 8
EDGE = 3
EXT = CAP + 2 * EDGE
ZERO = EXT
EPS = 1e-05
MESH = pl.DeviceIdType.MESH
BF = jnp.bfloat16
F32 = jnp.float32
OFFSETS = [(i, j, k) for i in range(3) for j in range(3) for k in range(3)]
PAIR_START = (2, 0, 3)


def lane_bits(shape):
    return lax.broadcasted_iota(jnp.int32, shape, len(shape) - 1) & 7


def group_sum(x):
    lane = lax.broadcasted_iota(jnp.int32, x.shape, 1)
    for step in (1, 2, 4):
        up = pltpu.roll(x, 128 - step, 1)
        down = pltpu.roll(x, step, 1)
        x = x + jnp.where((lane & step) == 0, up, down)
    return x


def group_total(x):
    return [
        jnp.sum(group_sum(x[:, h * 128 : (h + 1) * 128]), axis=0, keepdims=True) for h in range(2)
    ]


def spread_lane(row, lane):
    wide = jnp.broadcast_to(row, (8, 128))
    return group_sum(jnp.where(lane_bits((8, 128)) == lane, wide, 0.0))[0:1]


def pack_lanes(parts):
    bits = lane_bits((1, 128))
    row = jnp.zeros((1, 128), F32)
    for c, part in parts.items():
        row = jnp.where(bits == c, part, row)
    return row


def kernel(
    nd, ns,
    feat, mask, counts, nbr, w1, w2, gains, cot,
    out, gfeat,
    xb, cb, hb, ga2, xe, ce, he, ge, fb, mrow, me_row, wv, sv, eo, wt1, wt2, sx, sc, sh, sg, sm, ob, og, stat, recv, slots,
    lsem, osem, ssem, rsem, hs, hr,
):
    region, sub = lax.axis_index("region"), lax.axis_index("sub")
    me = region * ns + sub
    nxt, prv = lax.rem(me + 1, nd), lax.rem(me + nd - 1, nd)

    def place(o):
        return (lax.div(o, ns), lax.rem(o, ns))

    loads = [
        pltpu.make_async_copy(feat, xb, lsem.at[0]),
        pltpu.make_async_copy(cot, cb, lsem.at[1]),
        pltpu.make_async_copy(w1, wt1, lsem.at[2]),
        pltpu.make_async_copy(w2, wt2, lsem.at[3]),
    ]
    for c in loads:
        c.start()

    barrier = pltpu.get_barrier_semaphore()

    def greet(t, c):
        pl.semaphore_signal(
            barrier, inc=1, device_id=place(lax.rem(me + t, nd)), device_id_type=MESH
        )
        return c

    lax.fori_loop(1, nd, greet, 0)

    live = jnp.clip(counts[me], EDGE + 1, CAP)
    before = jnp.clip(counts[prv], EDGE + 1, CAP) - EDGE

    def place_slot(b, c):
        for o in range(27):
            name = nbr[b, o]
            owner = name >> 3
            inside = name & 7
            slot = jnp.where(
                owner == me, inside, jnp.where(owner < me, CAP + inside - before, CAP + EDGE + inside)
            )
            slots[b, o] = jnp.where(name < 0, ZERO, jnp.clip(slot, 0, ZERO))
        return c

    lax.fori_loop(0, CAP, place_slot, 0)

    eye = (
        lax.broadcasted_iota(jnp.int32, (128, 128), 0)
        == lax.broadcasted_iota(jnp.int32, (128, 128), 1)
    ).astype(F32)
    ones = jnp.ones((128, 128), BF)

    def wide(rows):
        return jnp.dot((eye * rows).astype(BF), ones, preferred_element_type=F32)

    def widen(b, c):
        wv[b] = wide(mrow[b])
        return c

    def widen_edge(e, c):
        wv[CAP + e] = wide(me_row[e])
        return c

    for b in range(CAP):
        alive = jnp.where(live > b, 1.0, 0.0).astype(F32)
        mrow[b] = mask[b : b + 1, :].astype(F32) * alive
    lax.fori_loop(0, CAP, widen, 0)

    def weight(b):
        w = wv[b]
        return jnp.concatenate([w, w], axis=1)

    sv[ZERO] = jnp.zeros((6, 4, 2, 16, 256), BF)

    def fold(x):
        return jnp.sum(x.reshape(16, 8, 256), axis=0)

    def send_row(k, row):
        stat[k] = row
        recv[k, me] = row

        def one(t, c):
            pltpu.make_async_remote_copy(
                src_ref=stat.at[k], dst_ref=recv.at[k, me], send_sem=ssem.at[k], recv_sem=rsem.at[k],
                device_id=place(lax.rem(me + t, nd)), device_id_type=MESH,
            ).start()
            return c

        lax.fori_loop(1, nd, one, 0)

    def all_rows(k):
        return pltpu.make_async_remote_copy(
            src_ref=recv.at[k, pl.ds(0, nd - 1)], dst_ref=recv.at[k, pl.ds(0, nd - 1)],
            send_sem=ssem.at[k], recv_sem=rsem.at[k], device_id=place(nxt), device_id_type=MESH,
        )

    def halo(k, staged, buffer, edges):
        to_next = pltpu.make_async_remote_copy(
            src_ref=staged, dst_ref=edges.at[0:EDGE],
            send_sem=hs.at[2 * k], recv_sem=hr.at[2 * k], device_id=place(nxt), device_id_type=MESH,
        )
        to_prev = pltpu.make_async_remote_copy(
            src_ref=buffer.at[0:EDGE], dst_ref=edges.at[EDGE : 2 * EDGE],
            send_sem=hs.at[2 * k + 1], recv_sem=hr.at[2 * k + 1], device_id=place(prv), device_id_type=MESH,
        )
        return to_next, to_prev

    def stage(staged, buffer):
        for e in range(EDGE):
            staged[e] = buffer[live - EDGE + e]

    count_rows = lax.fori_loop(
        0, CAP, lambda b, a: a + jnp.sum(wv[b].reshape(16, 8, 128), axis=0), jnp.zeros((8, 128), F32)
    )
    local_n = jnp.sum(count_rows, axis=0, keepdims=True) * GC

    def local_stats(value):
        total = lax.fori_loop(
            0, CAP, lambda b, a: a + fold(value(b) * weight(b)), jnp.zeros((8, 256), F32)
        )
        means = [s / jnp.maximum(local_n, 1.0) for s in group_total(total)]
        mean = jnp.concatenate(means, axis=1)

        def squares(b, a):
            d = value(b) - mean
            return a + fold(d * d * weight(b))

        m2 = group_total(lax.fori_loop(0, CAP, squares, jnp.zeros((8, 256), F32)))
        return pack_lanes({0: means[0], 1: m2[0], 2: means[1], 3: m2[1], 4: local_n, 6: local_n})

    def combine(k):
        rows = recv[k]
        total = jnp.sum(rows, axis=0)
        shifted = pltpu.roll(rows, 124, 2)
        weighted = jnp.sum(rows * shifted, axis=0)
        n = spread_lane(total, 4)
        means = [spread_lane(weighted, 2 * h) / n for h in range(2)]
        bits = lane_bits((1, 128))
        mean_row = jnp.where(bits == 0, means[0], jnp.where(bits == 2, means[1], 0.0))
        d = rows - mean_row
        between = jnp.sum(d * d * shifted, axis=0)
        invs = [
            lax.rsqrt((spread_lane(total, 2 * h + 1) + spread_lane(between, 2 * h)) / n + EPS)
            for h in range(2)
        ]
        return jnp.concatenate(means, axis=1), jnp.concatenate(invs, axis=1), n

    def back_row(sums):
        first, second = group_total(sums[0]), group_total(sums[1])
        return pack_lanes({0: first[0], 1: second[0], 2: first[1], 3: second[1]})

    def back_means(k, n):
        total = jnp.sum(recv[k], axis=0)
        first = jnp.concatenate([spread_lane(total, 0) / n, spread_lane(total, 2) / n], axis=1)
        second = jnp.concatenate([spread_lane(total, 1) / n, spread_lane(total, 3) / n], axis=1)
        return first, second

    def put_variants(s, a):
        a = a.reshape(16, 8, 256)
        for v, shift in enumerate((1, 0, 7)):
            q = (pltpu.roll(a, shift, 1) if shift else a).reshape(4, 4, 8, 256)
            sv[s, 2 * v] = q.reshape(4, 2, 16, 256).astype(BF)
            y = jnp.concatenate([q[:, 3:4], q[:, 0:3]], axis=1)
            sv[s, 2 * v + 1] = y.reshape(4, 2, 16, 256).astype(BF)

    row = lax.broadcasted_iota(jnp.int32, (16, 256), 0)
    z_first, z_last, upper = (row & 7) == 0, (row & 7) == 7, row < 8

    def gather(b, c):
        for v in range(3):
            for i in range(3):
                xs = (slice(3, 4), slice(0, 4), slice(0, 1))[i]
                xd = (slice(0, 1), slice(1, 5), slice(5, 6))[i]

                def load(j, parity, pairs):
                    here = sv[slots[b, i * 9 + j * 3 + 1], 2 * v + parity, xs, pairs]
                    if v == 1:
                        return here
                    there = sv[slots[b, i * 9 + j * 3 + v], 2 * v + parity, xs, pairs]
                    edge = jnp.broadcast_to(z_first if v == 0 else z_last, here.shape)
                    return jnp.where(edge, there, here)

                eo[b, v, xd, 0:2] = load(1, 0, slice(0, 2))
                wrap = load(1, 1, slice(0, 1))
                half = jnp.broadcast_to(upper, wrap.shape)
                eo[b, v, xd, 2:3] = jnp.where(half, load(0, 1, slice(0, 1)), wrap)
                eo[b, v, xd, 3:4] = load(1, 1, slice(1, 2))
                eo[b, v, xd, 4:5] = jnp.where(half, wrap, load(2, 1, slice(0, 1)))
        return c

    def operand(o):
        i, j, k = OFFSETS[o]
        tiles = eo[:, k, i : i + 4, PAIR_START[j] : PAIR_START[j] + 2]
        return tiles.reshape(CAP * 128, 256)

    def conv(weights):
        lax.fori_loop(0, CAP, gather, 0)
        acc = None
        for o in range(27):
            part = jnp.dot(
                operand(o), weights[o * 256 : (o + 1) * 256, :], preferred_element_type=F32
            )
            acc = part if acc is None else acc + part
        return acc.reshape(CAP, 128, 256)

    def conv_back(weights):
        lax.fori_loop(0, CAP, gather, 0)
        acc = None
        for o in range(27):
            part = lax.dot_general(
                operand(o), weights[(26 - o) * 256 : (27 - o) * 256, :],
                (((1,), (1,)), ((), ())), preferred_element_type=F32,
            )
            acc = part if acc is None else acc + part
        return acc.reshape(CAP, 128, 256)

    gain1, bias1, gain2, bias2 = (gains[r : r + 1, :] for r in range(4))

    loads[0].wait()
    stage(sx, xb)
    stage(sm, mrow)
    loads[1].wait()
    stage(sc, cb)

    def inputs(b):
        return xb[b].astype(F32) * weight(b)

    first_row = local_stats(inputs)

    pl.semaphore_wait(barrier, nd - 1)

    send_row(0, first_row)
    mask_halo, feat_halo, cot_halo = halo(0, sm, mrow, me_row), halo(1, sx, xb, xe), halo(2, sc, cb, ce)
    for pair in (mask_halo, feat_halo, cot_halo):
        for c in pair:
            c.start()

    for c in mask_halo:
        c.wait_recv()
    lax.fori_loop(0, 2 * EDGE, widen_edge, 0)
    for c in feat_halo:
        c.wait_recv()
    all_rows(0).wait_recv()
    mean1, inv1, n = combine(0)

    def both(body, local, edge):
        lax.fori_loop(0, CAP, lambda b, c: body(b, *(r[b] for r in local)) or c, 0)
        lax.fori_loop(0, 2 * EDGE, lambda e, c: body(CAP + e, *(r[e] for r in edge)) or c, 0)

    def first_act(s, x):
        w = weight(s)
        normed = (x.astype(F32) * w - mean1) * inv1
        pre = normed * gain1 + bias1
        put_variants(s, pre * jax.nn.sigmoid(pre) * w)

    both(first_act, (xb,), (xe,))
    loads[2].wait()
    fb[...] = conv(wt1)

    def keep_hidden(b, c):
        hb[b] = (fb[b] * weight(b)).astype(BF)
        return c

    lax.fori_loop(0, CAP, keep_hidden, 0)
    stage(sh, hb)
    hidden_halo = halo(3, sh, hb, he)
    send_row(1, local_stats(lambda b: hb[b].astype(F32)))
    for c in hidden_halo:
        c.start()

    for c in cot_halo:
        c.wait_recv()

    def grad_branch(s, g):
        put_variants(s, g.astype(F32) * weight(s))

    both(grad_branch, (cb,), (ce,))
    loads[3].wait()
    ga2[...] = conv_back(wt2)
    stage(sg, ga2)
    grad_halo = halo(4, sg, ga2, ge)
    for c in grad_halo:
        c.start()

    all_rows(1).wait_recv()
    mean2, inv2, _ = combine(1)

    def slope_of(pre, s):
        return s * (1.0 + pre * (1.0 - s))

    def second_local(b, sums):
        w = weight(b)
        normed = (hb[b].astype(F32) - mean2) * inv2
        pre = normed * gain2 + bias2
        s = jax.nn.sigmoid(pre)
        put_variants(b, pre * s * w)
        scaled = ga2[b] * slope_of(pre, s) * w * gain2
        return sums[0] + fold(scaled * w), sums[1] + fold(scaled * normed * w)

    zeros = jnp.zeros((8, 256), F32)
    send_row(2, back_row(lax.fori_loop(0, CAP, second_local, (zeros, zeros))))
    for c in hidden_halo:
        c.wait_recv()

    def second_edge(e, c):
        s = CAP + e
        w = weight(s)
        pre = (he[e].astype(F32) - mean2) * inv2 * gain2 + bias2
        put_variants(s, pre * jax.nn.sigmoid(pre) * w)
        return c

    lax.fori_loop(0, 2 * EDGE, second_edge, 0)
    fb[...] = conv(wt2)

    def finish(b, c):
        w = weight(b)
        ob[b] = ((xb[b].astype(F32) * w + fb[b]) * w).astype(BF)
        return c

    lax.fori_loop(0, CAP, finish, 0)
    store_out = pltpu.make_async_copy(ob, out, osem.at[0])
    store_out.start()

    for c in grad_halo:
        c.wait_recv()
    all_rows(2).wait_recv()
    first2, second2 = back_means(2, n)

    def grad_hidden(s, h, g):
        w = weight(s)
        normed = (h.astype(F32) - mean2) * inv2
        pre = normed * gain2 + bias2
        scaled = g * slope_of(pre, jax.nn.sigmoid(pre)) * w * gain2
        put_variants(s, inv2 * (scaled - first2 - normed * second2) * w)

    both(grad_hidden, (hb, ga2), (he, ge))
    fb[...] = conv_back(wt1)

    def first_back(b, sums):
        w = weight(b)
        normed = (xb[b].astype(F32) * w - mean1) * inv1
        pre = normed * gain1 + bias1
        scaled = fb[b] * slope_of(pre, jax.nn.sigmoid(pre)) * w * gain1
        fb[b] = scaled
        return sums[0] + fold(scaled * w), sums[1] + fold(scaled * normed * w)

    send_row(3, back_row(lax.fori_loop(0, CAP, first_back, (zeros, zeros))))
    all_rows(3).wait_recv()
    first1, second1 = back_means(3, n)

    def grad_features(b, c):
        w = weight(b)
        normed = (xb[b].astype(F32) * w - mean1) * inv1
        grad = inv1 * (fb[b] - first1 - normed * second1)
        og[b] = ((cb[b].astype(F32) + grad) * w).astype(BF)
        return c

    lax.fori_loop(0, CAP, grad_features, 0)
    store_grad = pltpu.make_async_copy(og, gfeat, osem.at[1])
    store_grad.start()

    for k in range(4):
        all_rows(k).wait_send()
    for pair in (mask_halo, feat_halo, cot_halo, hidden_halo, grad_halo):
        for c in pair:
            c.wait_send()
    store_out.wait()
    store_grad.wait()


def solution(mesh):
    ns = mesh.shape["sub"]
    nd = mesh.shape["region"] * ns

    def on_device(
        features, voxel_mask, counts, neighbors, w_first, w_second,
        gain_first, bias_first, gain_second, bias_second, cotangent,
    ):
        gains = jnp.stack([gain_first, bias_first, gain_second, bias_second])
        vmem = pl.BlockSpec(memory_space=pltpu.VMEM)
        smem = pl.BlockSpec(memory_space=pltpu.SMEM)
        hbm = pl.BlockSpec(memory_space=pl.ANY)
        shape = features.shape
        dma = pltpu.SemaphoreType.DMA
        return pl.pallas_call(
            functools.partial(kernel, nd, ns),
            out_shape=(jax.ShapeDtypeStruct(shape, BF), jax.ShapeDtypeStruct(shape, BF)),
            in_specs=[hbm, vmem, smem, smem, hbm, hbm, vmem, hbm],
            out_specs=(hbm, hbm),
            scratch_shapes=[
                pltpu.VMEM((CAP, 128, 256), BF),
                pltpu.VMEM((CAP, 128, 256), BF),
                pltpu.VMEM((CAP, 128, 256), BF),
                pltpu.VMEM((CAP, 128, 256), F32),
                pltpu.VMEM((2 * EDGE, 128, 256), BF),
                pltpu.VMEM((2 * EDGE, 128, 256), BF),
                pltpu.VMEM((2 * EDGE, 128, 256), BF),
                pltpu.VMEM((2 * EDGE, 128, 256), F32),
                pltpu.VMEM((CAP, 128, 256), F32),
                pltpu.VMEM((CAP, 1, 128), F32),
                pltpu.VMEM((2 * EDGE, 1, 128), F32),
                pltpu.VMEM((EXT, 128, 128), F32),
                pltpu.VMEM((EXT + 1, 6, 4, 2, 16, 256), BF),
                pltpu.VMEM((CAP, 3, 6, 5, 16, 256), BF),
                pltpu.VMEM((6912, 256), BF),
                pltpu.VMEM((6912, 256), BF),
                pltpu.VMEM((EDGE, 128, 256), BF),
                pltpu.VMEM((EDGE, 128, 256), BF),
                pltpu.VMEM((EDGE, 128, 256), BF),
                pltpu.VMEM((EDGE, 128, 256), F32),
                pltpu.VMEM((EDGE, 1, 128), F32),
                pltpu.VMEM((CAP, 128, 256), BF),
                pltpu.VMEM((CAP, 128, 256), BF),
                pltpu.VMEM((4, 1, 128), F32),
                pltpu.VMEM((4, nd, 1, 128), F32),
                pltpu.SMEM((CAP, 27), jnp.int32),
                dma((4,)),
                dma((2,)),
                dma((4,)),
                dma((4,)),
                dma((10,)),
                dma((10,)),
            ],
            compiler_params=pltpu.CompilerParams(
                collective_id=0, has_side_effects=True, vmem_limit_bytes=56 * 2**20
            ),
        )(features, voxel_mask, counts, neighbors, w_first, w_second, gains, cotangent)

    bricks = P(("region", "sub"), None, None)
    rows = P(("region", "sub"), None)
    return jax.shard_map(
        on_device,
        mesh=mesh,
        in_specs=(bricks, rows, P(), rows, P(), P(), P(), P(), P(), P(), bricks),
        out_specs=(bricks, bricks),
        check_vma=False,
    )
```

```python
import functools

import jax
import jax.numpy as jnp
from jax import lax
from jax.experimental import pallas as pl
from jax.experimental.pallas import tpu as pltpu
from jax.sharding import PartitionSpec as P

GC = 8
CAP = 8
EDGE = 3
EXT = CAP + 2 * EDGE
ZERO = EXT
EPS = 1e-05
HALF = CAP // 2
MESH = pl.DeviceIdType.MESH
BF = jnp.bfloat16
F32 = jnp.float32
OFFSETS = [(i, j, k) for i in range(3) for j in range(3) for k in range(3)]
PAIR_START = (2, 0, 3)


def hops(step, size):
    return min(step % size, -step % size)


def far_first(nd):
    steps = [(x, c, y, z) for x in range(4) for c in range(2) for y in range(4) for z in range(4)]
    return sorted(steps[1:], key=lambda s: -hops(s[0], 4) - hops(s[2], 4) - hops(s[3], 4))


def lane_bits(shape):
    return lax.broadcasted_iota(jnp.int32, shape, len(shape) - 1) & 7


def group_sum(x):
    lane = lax.broadcasted_iota(jnp.int32, x.shape, 1)
    for step in (1, 2, 4):
        up = pltpu.roll(x, 128 - step, 1)
        down = pltpu.roll(x, step, 1)
        x = x + jnp.where((lane & step) == 0, up, down)
    return x


def group_total(x):
    return [
        jnp.sum(group_sum(x[:, h * 128 : (h + 1) * 128]), axis=0, keepdims=True) for h in range(2)
    ]


def spread_lane(row, lane):
    wide = jnp.broadcast_to(row, (8, 128))
    return group_sum(jnp.where(lane_bits((8, 128)) == lane, wide, 0.0))[0:1]


def roll_row(row, step):
    return pltpu.roll(jnp.broadcast_to(row, (8, 128)), step, 1)[0:1]


def merge(rows):
    total = jnp.sum(rows, axis=0)
    counts = pltpu.roll(rows, 124, 2)
    weighted = jnp.sum(rows * counts, axis=0)
    n = spread_lane(total, 4)
    bits = lane_bits((1, 128))
    is_mean = (bits == 0) | (bits == 2)
    mean = jnp.where(is_mean, weighted / jnp.maximum(n, 1.0), 0.0)
    d = rows - mean
    between = jnp.where(is_mean, jnp.sum(d * d * counts, axis=0), 0.0)
    return jnp.where(is_mean, mean, total + roll_row(between, 1))


def pack_lanes(parts):
    bits = lane_bits((1, 128))
    row = jnp.zeros((1, 128), F32)
    for c, part in parts.items():
        row = jnp.where(bits == c, part, row)
    return row


def kernel(
    nd, ns,
    feat, mask, counts, nbr, w1, w2, gain1_ref, bias1_ref, gain2_ref, bias2_ref, cot,
    out, gfeat,
    xb, cb, hb, ga2, xe, ce, he, ge, fb, sl, fe, mrow, me_row, wv, sv, sw, eo, ep, wt1, wt2,
    sx, sc, sh, sg, sm, accs, stat, first, recv, rowa, rowb, slots,
    lsem, ssem, rsem, sas, sar, sbs, sbr, hs, hr,
):
    region, sub = lax.axis_index("region"), lax.axis_index("sub")
    me = region * ns + sub
    nxt, prv = lax.rem(me + 1, nd), lax.rem(me + nd - 1, nd)

    def place(o):
        return (lax.div(o, ns), lax.rem(o, ns))

    loads = [
        pltpu.make_async_copy(feat, xb, lsem.at[0]),
        pltpu.make_async_copy(cot, cb, lsem.at[1]),
        pltpu.make_async_copy(w1, wt1, lsem.at[2]),
        pltpu.make_async_copy(w2, wt2, lsem.at[3]),
    ]
    for c in loads:
        c.start()

    barrier = pltpu.get_barrier_semaphore()

    def greet(t, c):
        pl.semaphore_signal(
            barrier, inc=1, device_id=place(lax.rem(me + t, nd)), device_id_type=MESH
        )
        return c

    lax.fori_loop(1, nd, greet, 0)

    live = jnp.clip(counts[me], EDGE + 1, CAP)
    before = jnp.clip(counts[prv], EDGE + 1, CAP) - EDGE

    def place_slot(b, c):
        for o in range(27):
            name = nbr[b, o]
            owner = name >> 3
            inside = name & 7
            slot = jnp.where(
                owner == me, inside, jnp.where(owner < me, CAP + inside - before, CAP + EDGE + inside)
            )
            slots[b, o] = jnp.where(name < 0, ZERO, jnp.clip(slot, 0, ZERO))
        return c

    lax.fori_loop(0, CAP, place_slot, 0)

    eye = (
        lax.broadcasted_iota(jnp.int32, (128, 128), 0)
        == lax.broadcasted_iota(jnp.int32, (128, 128), 1)
    ).astype(F32)
    ones = jnp.ones((128, 128), BF)

    def wide(rows):
        return jnp.dot((eye * rows).astype(BF), ones, preferred_element_type=F32)

    def widen(b, c):
        wv[b] = wide(mrow[b])
        return c

    def widen_edge(e, c):
        wv[CAP + e] = wide(me_row[e])
        return c

    for b in range(CAP):
        alive = jnp.where(live > b, 1.0, 0.0).astype(F32)
        mrow[b] = mask[b : b + 1, :].astype(F32) * alive
    lax.fori_loop(0, CAP, widen, 0)

    def weight(b):
        w = wv[b]
        return jnp.concatenate([w, w], axis=1)

    for bank in (sv, sw):
        bank[ZERO] = jnp.zeros((6, 4, 2, 16, 256), BF)

    def fold(x):
        return jnp.sum(x.reshape(16, 8, 256), axis=0)

    def put_row(src, dst, send, recv_sem, target):
        pltpu.make_async_remote_copy(
            src_ref=src, dst_ref=dst, send_sem=send, recv_sem=recv_sem,
            device_id=target, device_id_type=MESH,
        ).start()

    def send_row(k, row):
        stat[k] = row
        recv[k, me] = row
        if nd == 128:
            xs = [lax.rem(lax.div(region, 2) + t, 4) * 2 for t in range(4)]
            cs = [lax.rem(region + t, 2) for t in range(2)]
            ys = [lax.rem(lax.div(sub, 4) + t, 4) * 4 for t in range(4)]
            zs = [lax.rem(sub + t, 4) for t in range(4)]
            for x, c, y, z in far_first(nd):
                target = (xs[x] + cs[c], ys[y] + zs[z])
                put_row(stat.at[k], recv.at[k, me], ssem.at[k], rsem.at[k], target)
        else:

            def one(t, c):
                target = place(lax.rem(me + t, nd))
                put_row(stat.at[k], recv.at[k, me], ssem.at[k], rsem.at[k], target)
                return c

            lax.fori_loop(1, nd, one, 0)

    def send_sub(k, row):
        first[k] = row
        rowa[k, sub] = row
        for t in range(1, ns):
            target = (region, lax.rem(sub + t, ns))
            put_row(first.at[k], rowa.at[k, sub], sas.at[k], sar.at[k], target)

    def send_region(k, combined):
        many(rowa, k, ns, sas, sar).wait_recv()
        row = combined(rowa[k])
        stat[k + 2] = row
        rowb[k, region] = row
        for t in range(1, nd // ns):
            target = (lax.rem(region + t, nd // ns), sub)
            put_row(stat.at[k + 2], rowb.at[k, region], sbs.at[k], sbr.at[k], target)

    def many(rows, k, size, send, recv_sem):
        block = rows.at[k, pl.ds(0, size - 1)]
        return pltpu.make_async_remote_copy(
            src_ref=block, dst_ref=block, send_sem=send.at[k], recv_sem=recv_sem.at[k],
            device_id=place(nxt), device_id_type=MESH,
        )

    def all_rows(k):
        return many(recv, k, nd, ssem, rsem)

    def halo(k, staged, buffer, edges):
        to_next = pltpu.make_async_remote_copy(
            src_ref=staged, dst_ref=edges.at[0:EDGE],
            send_sem=hs.at[2 * k], recv_sem=hr.at[2 * k], device_id=place(nxt), device_id_type=MESH,
        )
        to_prev = pltpu.make_async_remote_copy(
            src_ref=buffer.at[0:EDGE], dst_ref=edges.at[EDGE : 2 * EDGE],
            send_sem=hs.at[2 * k + 1], recv_sem=hr.at[2 * k + 1], device_id=place(prv), device_id_type=MESH,
        )
        return to_next, to_prev

    def stage(staged, buffer):
        for e in range(EDGE):
            staged[e] = buffer[live - EDGE + e]

    count_rows = lax.fori_loop(
        0, CAP, lambda b, a: a + jnp.sum(wv[b].reshape(16, 8, 128), axis=0), jnp.zeros((8, 128), F32)
    )
    local_n = jnp.sum(count_rows, axis=0, keepdims=True) * GC

    def local_sum(value):
        return lax.fori_loop(
            0, CAP, lambda b, a: a + fold(value(b) * weight(b)), jnp.zeros((8, 256), F32)
        )

    def local_stats(value, total):
        means = [s / jnp.maximum(local_n, 1.0) for s in group_total(total)]
        mean = jnp.concatenate(means, axis=1)

        def squares(b, a):
            d = value(b) - mean
            return a + fold(d * d * weight(b))

        m2 = group_total(lax.fori_loop(0, CAP, squares, jnp.zeros((8, 256), F32)))
        return pack_lanes({0: means[0], 1: m2[0], 2: means[1], 3: m2[1], 4: local_n, 6: local_n})

    def combine(rows):
        row = merge(rows)
        n = spread_lane(row, 4)
        mean = jnp.concatenate([spread_lane(row, 0), spread_lane(row, 2)], axis=1)
        spread = jnp.concatenate([spread_lane(row, 1) / n, spread_lane(row, 3) / n], axis=1)
        return mean, lax.rsqrt(spread + EPS), n

    def back_row(sums):
        first, second = group_total(sums[0]), group_total(sums[1])
        return pack_lanes({0: first[0], 1: second[0], 2: first[1], 3: second[1]})

    def back_means(rows, n):
        total = jnp.sum(rows, axis=0)
        first = jnp.concatenate([spread_lane(total, 0) / n, spread_lane(total, 2) / n], axis=1)
        second = jnp.concatenate([spread_lane(total, 1) / n, spread_lane(total, 3) / n], axis=1)
        return first, second

    def put_variants(bank, s, a):
        a = a.reshape(16, 8, 256)
        for v, shift in enumerate((1, 0, 7)):
            q = (pltpu.roll(a, shift, 1) if shift else a).reshape(4, 4, 8, 256)
            bank[s, 2 * v] = q.reshape(4, 2, 16, 256).astype(BF)
            y = jnp.concatenate([q[:, 3:4], q[:, 0:3]], axis=1)
            bank[s, 2 * v + 1] = y.reshape(4, 2, 16, 256).astype(BF)

    row = lax.broadcasted_iota(jnp.int32, (16, 256), 0)
    z_first, z_last, upper = (row & 7) == 0, (row & 7) == 7, row < 8

    def gather(bank, b, to, at, v, i):
        xs = (slice(3, 4), slice(0, 4), slice(0, 1))[i]
        xd = (slice(0, 1), slice(1, 5), slice(5, 6))[i]

        def load(j, parity, pairs):
            here = bank[slots[b, i * 9 + j * 3 + 1], 2 * v + parity, xs, pairs]
            if v == 1:
                return here
            there = bank[slots[b, i * 9 + j * 3 + v], 2 * v + parity, xs, pairs]
            edge = jnp.broadcast_to(z_first if v == 0 else z_last, here.shape)
            return jnp.where(edge, there, here)

        to[at, v, xd, 0:2] = load(1, 0, slice(0, 2))
        wrap = load(1, 1, slice(0, 1))
        half = jnp.broadcast_to(upper, wrap.shape)
        to[at, v, xd, 2:3] = jnp.where(half, load(0, 1, slice(0, 1)), wrap)
        to[at, v, xd, 3:4] = load(1, 1, slice(1, 2))
        to[at, v, xd, 4:5] = jnp.where(half, wrap, load(2, 1, slice(0, 1)))

    def gather_brick(bank, to):
        def one(b, c):
            for v in range(3):
                for i in range(3):
                    gather(bank, b, to, b, v, i)
            return c

        return one

    def product(tiles, weights, back, pieces):
        acc, done = None, 0
        for o, (i, j, k) in enumerate(OFFSETS):
            left = tiles[:, k, i : i + 4, PAIR_START[j] : PAIR_START[j] + 2].reshape(HALF * 128, 256)
            if back:
                block = weights[(26 - o) * 256 : (27 - o) * 256, :]
                part = lax.dot_general(
                    left, block, (((1,), (1,)), ((), ())), preferred_element_type=F32
                )
            else:
                part = jnp.dot(
                    left, weights[o * 256 : (o + 1) * 256, :], preferred_element_type=F32
                )
            acc = part if acc is None else acc + part
            while done * 27 < len(pieces) * (o + 1):
                pieces[done]()
                done += 1
        return acc.reshape(HALF, 128, 256)

    def conv(bank, weights, back, into, between=None, early=None):
        lax.fori_loop(0, HALF, gather_brick(bank, eo), 0)
        pieces = [
            functools.partial(gather, bank, HALF + b, ep, b, v, i)
            for b in range(HALF) for v in range(3) for i in range(3)
        ]
        into[0:HALF] = product(eo, weights, back, pieces)
        if between is not None:
            between()
        pieces = [functools.partial(early, b) for b in range(HALF)] if early is not None else []
        into[HALF:CAP] = product(ep, weights, back, pieces)

    gain1, bias1, gain2, bias2 = gain1_ref[...], bias1_ref[...], gain2_ref[...], bias2_ref[...]

    loads[0].wait()
    stage(sx, xb)
    stage(sm, mrow)

    def inputs(b):
        return xb[b].astype(F32) * weight(b)

    first_row = local_stats(inputs, local_sum(inputs))
    loads[1].wait()
    stage(sc, cb)

    def both(body, local, edge):
        lax.fori_loop(0, CAP, lambda b, c: body(b, *(r[b] for r in local)) or c, 0)
        lax.fori_loop(0, 2 * EDGE, lambda e, c: body(CAP + e, *(r[e] for r in edge)) or c, 0)

    def grad_branch(s, g):
        put_variants(sw, s, g.astype(F32) * weight(s))

    lax.fori_loop(0, CAP, lambda b, c: grad_branch(b, cb[b]) or c, 0)

    pl.semaphore_wait(barrier, nd - 1)

    mask_halo, feat_halo = halo(0, sm, mrow, me_row), halo(1, sx, xb, xe)
    cot_halo = halo(2, sc, cb, ce)
    for pair in (mask_halo, feat_halo):
        for c in pair:
            c.start()
    send_row(0, first_row)
    for c in cot_halo:
        c.start()

    for c in mask_halo:
        c.wait_recv()
    lax.fori_loop(0, 2 * EDGE, widen_edge, 0)
    all_rows(0).wait_recv()
    mean1, inv1, n = combine(recv[0])

    def first_act(s, x):
        w = weight(s)
        normed = (x.astype(F32) * w - mean1) * inv1
        pre = normed * gain1 + bias1
        put_variants(sv, s, pre * jax.nn.sigmoid(pre) * w)

    lax.fori_loop(0, CAP, lambda b, c: first_act(b, xb[b]) or c, 0)
    for c in feat_halo:
        c.wait_recv()
    lax.fori_loop(0, 2 * EDGE, lambda e, c: first_act(CAP + e, xe[e]) or c, 0)
    loads[2].wait()

    zeros = jnp.zeros((8, 256), F32)
    accs[0] = zeros
    accs[1] = zeros

    def keep_hidden(b, c=0):
        w = weight(b)
        h = (fb[b] * w).astype(BF)
        hb[b] = h
        accs[0] += fold(h.astype(F32) * w)
        return c

    conv(sv, wt1, False, fb, early=keep_hidden)
    lax.fori_loop(HALF, CAP, keep_hidden, 0)
    stage(sh, hb)
    hidden_halo = halo(3, sh, hb, he)
    send_sub(0, local_stats(lambda b: hb[b].astype(F32), accs[0]))
    for c in hidden_halo:
        c.start()

    for c in cot_halo:
        c.wait_recv()
    lax.fori_loop(0, 2 * EDGE, lambda e, c: grad_branch(CAP + e, ce[e]) or c, 0)
    loads[3].wait()
    conv(sw, wt2, True, ga2, between=lambda: send_region(0, merge))
    stage(sg, ga2)
    grad_halo = halo(4, sg, ga2, ge)
    for c in grad_halo:
        c.start()

    many(rowb, 0, nd // ns, sbs, sbr).wait_recv()
    mean2, inv2, _ = combine(rowb[0])

    def slope_of(pre, s):
        return s * (1.0 + pre * (1.0 - s))

    def second_local(b, sums):
        w = weight(b)
        normed = (hb[b].astype(F32) - mean2) * inv2
        pre = normed * gain2 + bias2
        s = jax.nn.sigmoid(pre)
        put_variants(sv, b, pre * s * w)
        scaled = ga2[b] * slope_of(pre, s) * w * gain2
        sl[b] = scaled
        return sums[0] + fold(scaled), sums[1] + fold(scaled * normed)

    send_sub(1, back_row(lax.fori_loop(0, CAP, second_local, (zeros, zeros))))
    for c in hidden_halo:
        c.wait_recv()

    def second_edge(e, c):
        s = CAP + e
        w = weight(s)
        pre = (he[e].astype(F32) - mean2) * inv2 * gain2 + bias2
        sig = jax.nn.sigmoid(pre)
        put_variants(sv, s, pre * sig * w)
        fe[e] = slope_of(pre, sig) * w * gain2
        return c

    lax.fori_loop(0, 2 * EDGE, second_edge, 0)

    def finish(b, c=0):
        w = weight(b)
        out[b] = ((xb[b].astype(F32) * w + fb[b]) * w).astype(BF)
        return c

    conv(
        sv, wt2, False, fb,
        between=lambda: send_region(1, lambda rows: jnp.sum(rows, axis=0)), early=finish,
    )
    lax.fori_loop(HALF, CAP, finish, 0)

    many(rowb, 1, nd // ns, sbs, sbr).wait_recv()
    first2, second2 = back_means(rowb[1], n)

    def grad_hidden(s, h, scaled):
        normed = (h.astype(F32) - mean2) * inv2
        put_variants(sw, s, inv2 * (scaled - first2 - normed * second2) * weight(s))

    lax.fori_loop(0, CAP, lambda b, c: grad_hidden(b, hb[b], sl[b]) or c, 0)
    for c in grad_halo:
        c.wait_recv()
    lax.fori_loop(0, 2 * EDGE, lambda e, c: grad_hidden(CAP + e, he[e], ge[e] * fe[e]) or c, 0)

    accs[0] = zeros
    accs[1] = zeros

    def first_back(b, c=0):
        w = weight(b)
        normed = (xb[b].astype(F32) * w - mean1) * inv1
        pre = normed * gain1 + bias1
        scaled = fb[b] * slope_of(pre, jax.nn.sigmoid(pre)) * w * gain1
        sl[b] = scaled
        accs[0] += fold(scaled)
        accs[1] += fold(scaled * normed)
        return c

    conv(sw, wt1, True, fb, early=first_back)
    lax.fori_loop(HALF, CAP, first_back, 0)
    send_row(1, back_row((accs[0], accs[1])))
    all_rows(1).wait_recv()
    first1, second1 = back_means(recv[1], n)

    def grad_features(b, c):
        w = weight(b)
        normed = (xb[b].astype(F32) * w - mean1) * inv1
        grad = inv1 * (sl[b] - first1 - normed * second1)
        gfeat[b] = ((cb[b].astype(F32) + grad) * w).astype(BF)
        return c

    lax.fori_loop(0, CAP, grad_features, 0)

    for k in range(2):
        all_rows(k).wait_send()
        many(rowa, k, ns, sas, sar).wait_send()
        many(rowb, k, nd // ns, sbs, sbr).wait_send()
    for pair in (mask_halo, feat_halo, cot_halo, hidden_halo, grad_halo):
        for c in pair:
            c.wait_send()


def hand_over(a, b, out_a, out_b, sem):
    copies = [
        pltpu.make_async_copy(a, out_a, sem.at[0]),
        pltpu.make_async_copy(b, out_b, sem.at[1]),
    ]
    for c in copies:
        c.start()
    for c in copies:
        c.wait()


def solution(mesh):
    ns = mesh.shape["sub"]
    nd = mesh.shape["region"] * ns

    def on_device(
        features, voxel_mask, counts, neighbors, w_first, w_second,
        gain_first, bias_first, gain_second, bias_second, cotangent,
    ):
        gains = [v.reshape(1, 256) for v in (gain_first, bias_first, gain_second, bias_second)]
        vmem = pl.BlockSpec(memory_space=pltpu.VMEM)
        smem = pl.BlockSpec(memory_space=pltpu.SMEM)
        hbm = pl.BlockSpec(memory_space=pl.ANY)
        shape = features.shape
        dma = pltpu.SemaphoreType.DMA
        results = pl.pallas_call(
            functools.partial(kernel, nd, ns),
            out_shape=(pltpu.VMEM(shape, BF), pltpu.VMEM(shape, BF)),
            in_specs=[hbm, vmem, smem, smem, hbm, hbm, vmem, vmem, vmem, vmem, hbm],
            out_specs=(vmem, vmem),
            scratch_shapes=[
                pltpu.VMEM((CAP, 128, 256), BF),
                pltpu.VMEM((CAP, 128, 256), BF),
                pltpu.VMEM((CAP, 128, 256), BF),
                pltpu.VMEM((CAP, 128, 256), F32),
                pltpu.VMEM((2 * EDGE, 128, 256), BF),
                pltpu.VMEM((2 * EDGE, 128, 256), BF),
                pltpu.VMEM((2 * EDGE, 128, 256), BF),
                pltpu.VMEM((2 * EDGE, 128, 256), F32),
                pltpu.VMEM((CAP, 128, 256), F32),
                pltpu.VMEM((CAP, 128, 256), F32),
                pltpu.VMEM((2 * EDGE, 128, 256), F32),
                pltpu.VMEM((CAP, 1, 128), F32),
                pltpu.VMEM((2 * EDGE, 1, 128), F32),
                pltpu.VMEM((EXT, 128, 128), F32),
                pltpu.VMEM((EXT + 1, 6, 4, 2, 16, 256), BF),
                pltpu.VMEM((EXT + 1, 6, 4, 2, 16, 256), BF),
                pltpu.VMEM((HALF, 3, 6, 5, 16, 256), BF),
                pltpu.VMEM((HALF, 3, 6, 5, 16, 256), BF),
                pltpu.VMEM((6912, 256), BF),
                pltpu.VMEM((6912, 256), BF),
                pltpu.VMEM((EDGE, 128, 256), BF),
                pltpu.VMEM((EDGE, 128, 256), BF),
                pltpu.VMEM((EDGE, 128, 256), BF),
                pltpu.VMEM((EDGE, 128, 256), F32),
                pltpu.VMEM((EDGE, 1, 128), F32),
                pltpu.VMEM((2, 8, 256), F32),
                pltpu.VMEM((4, 1, 128), F32),
                pltpu.VMEM((2, 1, 128), F32),
                pltpu.VMEM((2, nd, 1, 128), F32),
                pltpu.VMEM((2, ns, 1, 128), F32),
                pltpu.VMEM((2, nd // ns, 1, 128), F32),
                pltpu.SMEM((CAP, 27), jnp.int32),
                dma((4,)),
                dma((2,)),
                dma((2,)),
                dma((2,)),
                dma((2,)),
                dma((2,)),
                dma((2,)),
                dma((10,)),
                dma((10,)),
            ],
            compiler_params=pltpu.CompilerParams(
                collective_id=0, has_side_effects=True, vmem_limit_bytes=56 * 2**20
            ),
        )(features, voxel_mask, counts, neighbors, w_first, w_second, *gains, cotangent)
        return tuple(results)

    bricks = P(("region", "sub"), None, None)
    rows = P(("region", "sub"), None)
    return jax.shard_map(
        on_device,
        mesh=mesh,
        in_specs=(bricks, rows, P(), rows, P(), P(), P(), P(), P(), P(), bricks),
        out_specs=(bricks, bricks),
        check_vma=False,
    )
```

```python
import functools

import jax
import jax.numpy as jnp
from jax import lax
from jax.experimental import pallas as pl
from jax.experimental.pallas import tpu as pltpu
from jax.sharding import PartitionSpec as P

GC = 8
CAP = 8
EDGE = 3
EXT = CAP + 2 * EDGE
ZERO = EXT
EPS = 1e-05
HALF = CAP // 2
MESH = pl.DeviceIdType.MESH
BF = jnp.bfloat16
F32 = jnp.float32
OFFSETS = [(i, j, k) for i in range(3) for j in range(3) for k in range(3)]
PAIR_START = (2, 0, 3)


def hops(step, size):
    return min(step % size, -step % size)


def far_first(nd):
    steps = [(x, c, y, z) for x in range(4) for c in range(2) for y in range(4) for z in range(4)]
    return sorted(steps[1:], key=lambda s: -hops(s[0], 4) - hops(s[2], 4) - hops(s[3], 4))


def lane_bits(shape):
    return lax.broadcasted_iota(jnp.int32, shape, len(shape) - 1) & 7


def group_sum(x):
    lane = lax.broadcasted_iota(jnp.int32, x.shape, 1)
    for step in (1, 2, 4):
        up = pltpu.roll(x, 128 - step, 1)
        down = pltpu.roll(x, step, 1)
        x = x + jnp.where((lane & step) == 0, up, down)
    return x


def group_total(x):
    return [
        jnp.sum(group_sum(x[:, h * 128 : (h + 1) * 128]), axis=0, keepdims=True) for h in range(2)
    ]


def spread_lane(row, lane):
    wide = jnp.broadcast_to(row, (8, 128))
    return group_sum(jnp.where(lane_bits((8, 128)) == lane, wide, 0.0))[0:1]


def roll_row(row, step):
    return pltpu.roll(jnp.broadcast_to(row, (8, 128)), step, 1)[0:1]


def merge(rows):
    total = jnp.sum(rows, axis=0)
    counts = pltpu.roll(rows, 124, 2)
    weighted = jnp.sum(rows * counts, axis=0)
    n = roll_row(total, 124)
    bits = lane_bits((1, 128))
    is_mean = (bits == 0) | (bits == 2)
    mean = jnp.where(is_mean, weighted / jnp.maximum(n, 1.0), 0.0)
    d = rows - mean
    between = jnp.where(is_mean, jnp.sum(d * d * counts, axis=0), 0.0)
    return jnp.where(is_mean, mean, total + roll_row(between, 1))


def pack_lanes(parts):
    bits = lane_bits((1, 128))
    row = jnp.zeros((1, 128), F32)
    for c, part in parts.items():
        row = jnp.where(bits == c, part, row)
    return row


def kernel(
    nd, ns,
    feat, mask, counts, nbr, w1, w2, gain1_ref, bias1_ref, gain2_ref, bias2_ref, cot,
    out, gfeat,
    xb, cb, hb, ga2, xe, ce, he, ge, fb, sl, mrow, me_row, wv, sv, sw, eo, ep, wt1, wt2,
    sx, sc, sh, rn, rp, sm, nb, accs, stat, first, recv, rowa, rowb, slots,
    lsem, ssem, rsem, sas, sar, sbs, sbr, hs, hr,
):
    region, sub = lax.axis_index("region"), lax.axis_index("sub")
    me = region * ns + sub
    nxt, prv = lax.rem(me + 1, nd), lax.rem(me + nd - 1, nd)

    def place(o):
        return (lax.div(o, ns), lax.rem(o, ns))

    loads = [
        pltpu.make_async_copy(feat, xb, lsem.at[0]),
        pltpu.make_async_copy(cot, cb, lsem.at[1]),
        pltpu.make_async_copy(w1, wt1, lsem.at[2]),
        pltpu.make_async_copy(w2, wt2, lsem.at[3]),
    ]
    for c in loads:
        c.start()

    barrier = pltpu.get_barrier_semaphore()

    if nd == 128:
        xs = [lax.rem(lax.div(region, 2) + t, 4) * 2 for t in range(4)]
        cs = [lax.rem(region + t, 2) for t in range(2)]
        ys = [lax.rem(lax.div(sub, 4) + t, 4) * 4 for t in range(4)]
        zs = [lax.rem(sub + t, 4) for t in range(4)]
        others = [(xs[x] + cs[c], ys[y] + zs[z]) for x, c, y, z in far_first(nd)]
    else:
        others = [place(lax.rem(me + t, nd)) for t in range(1, nd)]
    for other in others:
        pl.semaphore_signal(barrier, inc=1, device_id=other, device_id_type=MESH)

    live = jnp.clip(counts[me], EDGE + 1, CAP)
    before = jnp.clip(counts[prv], EDGE + 1, CAP) - EDGE

    def place_slot(b, c):
        for o in range(27):
            name = nbr[b, o]
            owner = name >> 3
            inside = name & 7
            slot = jnp.where(
                owner == me, inside, jnp.where(owner < me, CAP + inside - before, CAP + EDGE + inside)
            )
            slots[b, o] = jnp.where(name < 0, ZERO, jnp.clip(slot, 0, ZERO))
        return c

    lax.fori_loop(0, CAP, place_slot, 0)

    eye = (
        lax.broadcasted_iota(jnp.int32, (128, 128), 0)
        == lax.broadcasted_iota(jnp.int32, (128, 128), 1)
    ).astype(F32)
    ones = jnp.ones((128, 128), BF)

    def wide(rows):
        return jnp.dot((eye * rows).astype(BF), ones, preferred_element_type=F32)

    def widen(b, c):
        wv[b] = wide(mrow[b])
        return c

    def widen_edge(e, c):
        wv[CAP + e] = wide(me_row[e])
        return c

    for b in range(CAP):
        alive = jnp.where(live > b, 1.0, 0.0).astype(F32)
        mrow[b] = mask[b : b + 1, :].astype(F32) * alive
    lax.fori_loop(0, CAP, widen, 0)

    def weight(b):
        w = wv[b]
        return jnp.concatenate([w, w], axis=1)

    for bank in (sv, sw):
        bank[ZERO] = jnp.zeros((6, 4, 2, 16, 256), BF)

    def fold(x):
        return jnp.sum(x.reshape(16, 8, 256), axis=0)

    def put_row(src, dst, send, recv_sem, target):
        pltpu.make_async_remote_copy(
            src_ref=src, dst_ref=dst, send_sem=send, recv_sem=recv_sem,
            device_id=target, device_id_type=MESH,
        ).start()

    def send_row(k, row):
        stat[k] = row
        recv[k, me] = row
        for other in others:
            put_row(stat.at[k], recv.at[k, me], ssem.at[k], rsem.at[k], other)

    def send_sub(k, row):
        first[k] = row
        rowa[k, sub] = row
        for t in range(1, ns):
            target = (region, lax.rem(sub + t, ns))
            put_row(first.at[k], rowa.at[k, sub], sas.at[k], sar.at[k], target)

    def send_region(k, combined):
        many(rowa, k, ns, sas, sar).wait_recv()
        row = combined(rowa[k])
        stat[k + 2] = row
        rowb[k, region] = row
        for t in range(1, nd // ns):
            target = (lax.rem(region + t, nd // ns), sub)
            put_row(stat.at[k + 2], rowb.at[k, region], sbs.at[k], sbr.at[k], target)

    def many(rows, k, size, send, recv_sem):
        block = rows.at[k, pl.ds(0, size - 1)]
        return pltpu.make_async_remote_copy(
            src_ref=block, dst_ref=block, send_sem=send.at[k], recv_sem=recv_sem.at[k],
            device_id=place(nxt), device_id_type=MESH,
        )

    def all_rows(k):
        return many(recv, k, nd, ssem, rsem)

    def exchange(k, ahead, back, edges, width):
        to_next = pltpu.make_async_remote_copy(
            src_ref=ahead, dst_ref=edges.at[0:width],
            send_sem=hs.at[2 * k], recv_sem=hr.at[2 * k], device_id=place(nxt), device_id_type=MESH,
        )
        to_prev = pltpu.make_async_remote_copy(
            src_ref=back, dst_ref=edges.at[width : 2 * width],
            send_sem=hs.at[2 * k + 1], recv_sem=hr.at[2 * k + 1], device_id=place(prv), device_id_type=MESH,
        )
        return to_next, to_prev

    def halo(k, staged, buffer, edges):
        return exchange(k, staged, buffer.at[0:EDGE], edges, EDGE)

    def stage(staged, buffer):
        for e in range(EDGE):
            staged[e] = buffer[live - EDGE + e]

    count_rows = lax.fori_loop(
        0, CAP, lambda b, a: a + jnp.sum(wv[b].reshape(16, 8, 128), axis=0), jnp.zeros((8, 128), F32)
    )
    local_n = jnp.sum(count_rows, axis=0, keepdims=True) * GC

    def local_sum(value):
        return lax.fori_loop(
            0, CAP, lambda b, a: a + fold(value(b) * weight(b)), jnp.zeros((8, 256), F32)
        )

    def local_stats(value, total):
        means = [s / jnp.maximum(local_n, 1.0) for s in group_total(total)]
        mean = jnp.concatenate(means, axis=1)

        def squares(b, a):
            d = value(b) - mean
            return a + fold(d * d * weight(b))

        m2 = group_total(lax.fori_loop(0, CAP, squares, jnp.zeros((8, 256), F32)))
        return pack_lanes({0: means[0], 1: m2[0], 2: means[1], 3: m2[1], 4: local_n, 6: local_n})

    def combine(rows):
        row = merge(rows)
        n = spread_lane(row, 4)
        mean = jnp.concatenate([spread_lane(row, 0), spread_lane(row, 2)], axis=1)
        spread = jnp.concatenate([spread_lane(row, 1) / n, spread_lane(row, 3) / n], axis=1)
        return mean, lax.rsqrt(spread + EPS), n

    def back_row(sums):
        first, second = group_total(sums[0]), group_total(sums[1])
        return pack_lanes({0: first[0], 1: second[0], 2: first[1], 3: second[1], 4: local_n})

    def back_means(row, n):
        first = jnp.concatenate([spread_lane(row, 0) / n, spread_lane(row, 2) / n], axis=1)
        second = jnp.concatenate([spread_lane(row, 1) / n, spread_lane(row, 3) / n], axis=1)
        return first, second

    def own_means(row):
        return back_means(row, jnp.maximum(spread_lane(row, 4), 1.0))

    def add_rows(rows):
        return jnp.sum(rows, axis=0)

    def put_variants(bank, s, a):
        a = a.reshape(16, 8, 256)
        for v, shift in enumerate((1, 0, 7)):
            q = (pltpu.roll(a, shift, 1) if shift else a).reshape(4, 4, 8, 256)
            bank[s, 2 * v] = q.reshape(4, 2, 16, 256).astype(BF)
            y = jnp.concatenate([q[:, 3:4], q[:, 0:3]], axis=1)
            bank[s, 2 * v + 1] = y.reshape(4, 2, 16, 256).astype(BF)

    row = lax.broadcasted_iota(jnp.int32, (16, 256), 0)
    z_first, z_last, upper = (row & 7) == 0, (row & 7) == 7, row < 8

    def gather(bank, b, to, at, v, i):
        xs = (slice(3, 4), slice(0, 4), slice(0, 1))[i]
        xd = (slice(0, 1), slice(1, 5), slice(5, 6))[i]

        def load(j, parity, pairs):
            here = bank[slots[b, i * 9 + j * 3 + 1], 2 * v + parity, xs, pairs]
            if v == 1:
                return here
            there = bank[slots[b, i * 9 + j * 3 + v], 2 * v + parity, xs, pairs]
            edge = jnp.broadcast_to(z_first if v == 0 else z_last, here.shape)
            return jnp.where(edge, there, here)

        to[at, v, xd, 0:2] = load(1, 0, slice(0, 2))
        wrap = load(1, 1, slice(0, 1))
        half = jnp.broadcast_to(upper, wrap.shape)
        to[at, v, xd, 2:3] = jnp.where(half, load(0, 1, slice(0, 1)), wrap)
        to[at, v, xd, 3:4] = load(1, 1, slice(1, 2))
        to[at, v, xd, 4:5] = jnp.where(half, wrap, load(2, 1, slice(0, 1)))

    def gather_brick(bank, to):
        def one(b, c):
            for v in range(3):
                for i in range(3):
                    gather(bank, b, to, b, v, i)
            return c

        return one

    def product(tiles, weights, back, pieces):
        acc, done = None, 0
        for o, (i, j, k) in enumerate(OFFSETS):
            left = tiles[:, k, i : i + 4, PAIR_START[j] : PAIR_START[j] + 2].reshape(HALF * 128, 256)
            if back:
                block = weights[(26 - o) * 256 : (27 - o) * 256, :]
                part = lax.dot_general(
                    left, block, (((1,), (1,)), ((), ())), preferred_element_type=F32
                )
            else:
                part = jnp.dot(
                    left, weights[o * 256 : (o + 1) * 256, :], preferred_element_type=F32
                )
            acc = part if acc is None else acc + part
            while done * 27 < len(pieces) * (o + 1):
                pieces[done]()
                done += 1
        return acc.reshape(HALF, 128, 256)

    def conv(bank, weights, back, into, between=None, early=None):
        lax.fori_loop(0, HALF, gather_brick(bank, eo), 0)
        pieces = [
            functools.partial(gather, bank, HALF + b, ep, b, v, i)
            for b in range(HALF) for v in range(3) for i in range(3)
        ]
        into[0:HALF] = product(eo, weights, back, pieces)
        if between is not None:
            between()
        pieces = [functools.partial(early, b) for b in range(HALF)] if early is not None else []
        into[HALF:CAP] = product(ep, weights, back, pieces)

    gain1, bias1, gain2, bias2 = gain1_ref[...], bias1_ref[...], gain2_ref[...], bias2_ref[...]

    loads[0].wait()
    stage(sx, xb)
    stage(sm, mrow)

    def inputs(b):
        return xb[b].astype(F32) * weight(b)

    first_row = local_stats(inputs, local_sum(inputs))
    loads[1].wait()
    stage(sc, cb)

    def both(body, local, edge):
        lax.fori_loop(0, CAP, lambda b, c: body(b, *(r[b] for r in local)) or c, 0)
        lax.fori_loop(0, 2 * EDGE, lambda e, c: body(CAP + e, *(r[e] for r in edge)) or c, 0)

    def grad_branch(s, g):
        put_variants(sw, s, g.astype(F32) * weight(s))

    lax.fori_loop(0, CAP, lambda b, c: grad_branch(b, cb[b]) or c, 0)

    pl.semaphore_wait(barrier, nd - 1)

    mask_halo, feat_halo = halo(0, sm, mrow, me_row), halo(1, sx, xb, xe)
    cot_halo = halo(2, sc, cb, ce)
    send_row(0, first_row)
    for pair in (mask_halo, feat_halo, cot_halo):
        for c in pair:
            c.start()

    for c in mask_halo:
        c.wait_recv()
    lax.fori_loop(0, 2 * EDGE, widen_edge, 0)
    all_rows(0).wait_recv()
    mean1, inv1, n = combine(recv[0])

    def first_act(s, x):
        w = weight(s)
        normed = (x.astype(F32) * w - mean1) * inv1
        pre = normed * gain1 + bias1
        put_variants(sv, s, pre * jax.nn.sigmoid(pre) * w)

    lax.fori_loop(0, CAP, lambda b, c: first_act(b, xb[b]) or c, 0)
    for c in feat_halo:
        c.wait_recv()
    lax.fori_loop(0, 2 * EDGE, lambda e, c: first_act(CAP + e, xe[e]) or c, 0)
    loads[2].wait()

    zeros = jnp.zeros((8, 256), F32)
    accs[0] = zeros
    accs[1] = zeros

    def keep_hidden(b, c=0):
        w = weight(b)
        h = (fb[b] * w).astype(BF)
        hb[b] = h
        accs[0] += fold(h.astype(F32) * w)
        return c

    conv(sv, wt1, False, fb, early=keep_hidden)
    lax.fori_loop(HALF, CAP, keep_hidden, 0)
    stage(sh, hb)
    hidden_halo = halo(3, sh, hb, he)
    send_sub(0, local_stats(lambda b: hb[b].astype(F32), accs[0]))
    for c in hidden_halo:
        c.start()

    for c in cot_halo:
        c.wait_recv()
    lax.fori_loop(0, 2 * EDGE, lambda e, c: grad_branch(CAP + e, ce[e]) or c, 0)
    loads[3].wait()
    conv(sw, wt2, True, ga2, between=lambda: send_region(0, merge))
    many(rowb, 0, nd // ns, sbs, sbr).wait_recv()
    mean2, inv2, _ = combine(rowb[0])

    def slope_of(pre, s):
        return s * (1.0 + pre * (1.0 - s))

    def second_local(b, sums):
        w = weight(b)
        normed = (hb[b].astype(F32) - mean2) * inv2
        pre = normed * gain2 + bias2
        s = jax.nn.sigmoid(pre)
        put_variants(sv, b, pre * s * w)
        scaled = ga2[b] * slope_of(pre, s) * w * gain2
        sl[b] = scaled
        return sums[0] + fold(scaled), sums[1] + fold(scaled * normed)

    own_row = back_row(lax.fori_loop(0, CAP, second_local, (zeros, zeros)))
    send_sub(1, own_row)

    own_first, own_second = own_means(own_row)

    def residual(b):
        normed = (hb[b].astype(F32) - mean2) * inv2
        return (sl[b] - own_first - normed * own_second).astype(BF)

    for e in range(EDGE):
        rp[e] = residual(e)
        rn[e] = residual(live - EDGE + e)
    grad_halo = exchange(4, rn, rp, ge, EDGE)
    means_halo = exchange(5, first.at[pl.ds(1, 1)], first.at[pl.ds(1, 1)], nb, 1)
    for pair in (means_halo, grad_halo):
        for c in pair:
            c.start()

    for c in hidden_halo:
        c.wait_recv()

    def second_edge(e, c):
        s = CAP + e
        w = weight(s)
        pre = (he[e].astype(F32) - mean2) * inv2 * gain2 + bias2
        put_variants(sv, s, pre * jax.nn.sigmoid(pre) * w)
        return c

    lax.fori_loop(0, 2 * EDGE, second_edge, 0)

    def finish(b, c=0):
        w = weight(b)
        out[b] = ((xb[b].astype(F32) * w + fb[b]) * w).astype(BF)
        return c

    conv(
        sv, wt2, False, fb,
        between=lambda: send_region(1, add_rows), early=finish,
    )
    lax.fori_loop(HALF, CAP, finish, 0)

    many(rowb, 1, nd // ns, sbs, sbr).wait_recv()
    first2, second2 = back_means(add_rows(rowb[1]), n)

    def grad_hidden(s, h, scaled, along_first, along_second):
        normed = (h.astype(F32) - mean2) * inv2
        grad = inv2 * (scaled - along_first - normed * along_second) * weight(s)
        put_variants(sw, s, grad)

    lax.fori_loop(0, CAP, lambda b, c: grad_hidden(b, hb[b], sl[b], first2, second2) or c, 0)
    for pair in (means_halo, grad_halo):
        for c in pair:
            c.wait_recv()
    for side in range(2):
        side_first, side_second = own_means(nb[side])
        side_first, side_second = first2 - side_first, second2 - side_second

        def edge_grad(e, c):
            grad_hidden(CAP + e, he[e], ge[e].astype(F32), side_first, side_second)
            return c

        lax.fori_loop(side * EDGE, (side + 1) * EDGE, edge_grad, 0)

    accs[0] = zeros
    accs[1] = zeros

    def first_back(b, c=0):
        w = weight(b)
        normed = (xb[b].astype(F32) * w - mean1) * inv1
        pre = normed * gain1 + bias1
        scaled = fb[b] * slope_of(pre, jax.nn.sigmoid(pre)) * w * gain1
        sl[b] = scaled
        accs[0] += fold(scaled)
        accs[1] += fold(scaled * normed)
        return c

    conv(sw, wt1, True, fb, early=first_back)
    lax.fori_loop(HALF, CAP, first_back, 0)
    send_row(1, back_row((accs[0], accs[1])))
    all_rows(1).wait_recv()
    first1, second1 = back_means(add_rows(recv[1]), n)

    def grad_features(b, c):
        w = weight(b)
        normed = (xb[b].astype(F32) * w - mean1) * inv1
        grad = inv1 * (sl[b] - first1 - normed * second1)
        gfeat[b] = ((cb[b].astype(F32) + grad) * w).astype(BF)
        return c

    lax.fori_loop(0, CAP, grad_features, 0)

    for k in range(2):
        all_rows(k).wait_send()
        many(rowa, k, ns, sas, sar).wait_send()
        many(rowb, k, nd // ns, sbs, sbr).wait_send()
    for pair in (mask_halo, feat_halo, cot_halo, hidden_halo, grad_halo, means_halo):
        for c in pair:
            c.wait_send()


def solution(mesh):
    ns = mesh.shape["sub"]
    nd = mesh.shape["region"] * ns

    def on_device(
        features, voxel_mask, counts, neighbors, w_first, w_second,
        gain_first, bias_first, gain_second, bias_second, cotangent,
    ):
        gains = [v.reshape(1, 256) for v in (gain_first, bias_first, gain_second, bias_second)]
        vmem = pl.BlockSpec(memory_space=pltpu.VMEM)
        smem = pl.BlockSpec(memory_space=pltpu.SMEM)
        hbm = pl.BlockSpec(memory_space=pl.ANY)
        shape = features.shape
        dma = pltpu.SemaphoreType.DMA
        results = pl.pallas_call(
            functools.partial(kernel, nd, ns),
            out_shape=(pltpu.VMEM(shape, BF), pltpu.VMEM(shape, BF)),
            in_specs=[hbm, vmem, smem, smem, hbm, hbm, vmem, vmem, vmem, vmem, hbm],
            out_specs=(vmem, vmem),
            scratch_shapes=[
                pltpu.VMEM((CAP, 128, 256), BF),
                pltpu.VMEM((CAP, 128, 256), BF),
                pltpu.VMEM((CAP, 128, 256), BF),
                pltpu.VMEM((CAP, 128, 256), F32),
                pltpu.VMEM((2 * EDGE, 128, 256), BF),
                pltpu.VMEM((2 * EDGE, 128, 256), BF),
                pltpu.VMEM((2 * EDGE, 128, 256), BF),
                pltpu.VMEM((2 * EDGE, 128, 256), BF),
                pltpu.VMEM((CAP, 128, 256), F32),
                pltpu.VMEM((CAP, 128, 256), F32),
                pltpu.VMEM((CAP, 1, 128), F32),
                pltpu.VMEM((2 * EDGE, 1, 128), F32),
                pltpu.VMEM((EXT, 128, 128), F32),
                pltpu.VMEM((EXT + 1, 6, 4, 2, 16, 256), BF),
                pltpu.VMEM((EXT + 1, 6, 4, 2, 16, 256), BF),
                pltpu.VMEM((HALF, 3, 6, 5, 16, 256), BF),
                pltpu.VMEM((HALF, 3, 6, 5, 16, 256), BF),
                pltpu.VMEM((6912, 256), BF),
                pltpu.VMEM((6912, 256), BF),
                pltpu.VMEM((EDGE, 128, 256), BF),
                pltpu.VMEM((EDGE, 128, 256), BF),
                pltpu.VMEM((EDGE, 128, 256), BF),
                pltpu.VMEM((EDGE, 128, 256), BF),
                pltpu.VMEM((EDGE, 128, 256), BF),
                pltpu.VMEM((EDGE, 1, 128), F32),
                pltpu.VMEM((2, 1, 128), F32),
                pltpu.VMEM((2, 8, 256), F32),
                pltpu.VMEM((4, 1, 128), F32),
                pltpu.VMEM((2, 1, 128), F32),
                pltpu.VMEM((2, nd, 1, 128), F32),
                pltpu.VMEM((2, ns, 1, 128), F32),
                pltpu.VMEM((2, nd // ns, 1, 128), F32),
                pltpu.SMEM((CAP, 27), jnp.int32),
                dma((4,)),
                dma((2,)),
                dma((2,)),
                dma((2,)),
                dma((2,)),
                dma((2,)),
                dma((2,)),
                dma((12,)),
                dma((12,)),
            ],
            compiler_params=pltpu.CompilerParams(
                collective_id=0, has_side_effects=True, vmem_limit_bytes=56 * 2**20
            ),
        )(features, voxel_mask, counts, neighbors, w_first, w_second, *gains, cotangent)
        return tuple(results)

    bricks = P(("region", "sub"), None, None)
    rows = P(("region", "sub"), None)
    return jax.shard_map(
        on_device,
        mesh=mesh,
        in_specs=(bricks, rows, P(), rows, P(), P(), P(), P(), P(), P(), bricks),
        out_specs=(bricks, bricks),
        check_vma=False,
    )
```

```python
import functools

import jax
import jax.numpy as jnp
from jax import lax
from jax.experimental import pallas as pl
from jax.experimental.pallas import tpu as pltpu
from jax.sharding import PartitionSpec as P

GC = 8
CAP = 8
EDGE = 3
EXT = CAP + 2 * EDGE
ZERO = EXT
EPS = 1e-05
HALF = CAP // 2
MESH = pl.DeviceIdType.MESH
BF = jnp.bfloat16
F32 = jnp.float32
OFFSETS = [(i, j, k) for i in range(3) for j in range(3) for k in range(3)]
PAIR_START = (2, 0, 3)


def hops(step, size):
    return min(step % size, -step % size)


def far_first(nd):
    steps = [(x, c, y, z) for x in range(4) for c in range(2) for y in range(4) for z in range(4)]
    return sorted(steps[1:], key=lambda s: -hops(s[0], 4) - hops(s[2], 4) - hops(s[3], 4))


def lane_bits(shape):
    return lax.broadcasted_iota(jnp.int32, shape, len(shape) - 1) & 7


def group_sum(x):
    lane = lax.broadcasted_iota(jnp.int32, x.shape, 1)
    for step in (1, 2, 4):
        up = pltpu.roll(x, 128 - step, 1)
        down = pltpu.roll(x, step, 1)
        x = x + jnp.where((lane & step) == 0, up, down)
    return x


def group_total(x):
    return [
        jnp.sum(group_sum(x[:, h * 128 : (h + 1) * 128]), axis=0, keepdims=True) for h in range(2)
    ]


def spread_lane(row, lane):
    wide = jnp.broadcast_to(row, (8, 128))
    return group_sum(jnp.where(lane_bits((8, 128)) == lane, wide, 0.0))[0:1]


def roll_row(row, step):
    return pltpu.roll(jnp.broadcast_to(row, (8, 128)), step, 1)[0:1]


def merge(rows):
    total = jnp.sum(rows, axis=0)
    counts = pltpu.roll(rows, 124, 2)
    weighted = jnp.sum(rows * counts, axis=0)
    n = roll_row(total, 124)
    bits = lane_bits((1, 128))
    is_mean = (bits == 0) | (bits == 2)
    mean = jnp.where(is_mean, weighted / jnp.maximum(n, 1.0), 0.0)
    d = rows - mean
    between = jnp.where(is_mean, jnp.sum(d * d * counts, axis=0), 0.0)
    return jnp.where(is_mean, mean, total + roll_row(between, 1))


def pack_lanes(parts):
    bits = lane_bits((1, 128))
    row = jnp.zeros((1, 128), F32)
    for c, part in parts.items():
        row = jnp.where(bits == c, part, row)
    return row


def kernel(
    nd, ns,
    feat, mask, counts, nbr, w1, w2, gain1_ref, bias1_ref, gain2_ref, bias2_ref, cot,
    out, gfeat,
    xb, cb, hb, ga2, xe, ce, he, ge, fb, sl, mrow, me_row, wv, sv, sw, eo, ep, wt1, wt2,
    sx, sc, sh, rn, rp, sm, nb, accs, stat, first, recv, rowa, rowb, slots,
    lsem, ssem, rsem, sas, sar, sbs, sbr, hs, hr,
):
    region, sub = lax.axis_index("region"), lax.axis_index("sub")
    me = region * ns + sub
    nxt, prv = lax.rem(me + 1, nd), lax.rem(me + nd - 1, nd)

    def place(o):
        return (lax.div(o, ns), lax.rem(o, ns))

    loads = [
        pltpu.make_async_copy(feat, xb, lsem.at[0]),
        pltpu.make_async_copy(cot, cb, lsem.at[1]),
        pltpu.make_async_copy(w1, wt1, lsem.at[2]),
        pltpu.make_async_copy(w2, wt2, lsem.at[3]),
    ]
    for c in loads:
        c.start()

    barrier = pltpu.get_barrier_semaphore()

    if nd == 128:
        xs = [lax.rem(lax.div(region, 2) + t, 4) * 2 for t in range(4)]
        cs = [lax.rem(region + t, 2) for t in range(2)]
        ys = [lax.rem(lax.div(sub, 4) + t, 4) * 4 for t in range(4)]
        zs = [lax.rem(sub + t, 4) for t in range(4)]
        others = [(xs[x] + cs[c], ys[y] + zs[z]) for x, c, y, z in far_first(nd)]
    else:
        others = [place(lax.rem(me + t, nd)) for t in range(1, nd)]
    for other in others:
        pl.semaphore_signal(barrier, inc=1, device_id=other, device_id_type=MESH)

    live = jnp.clip(counts[me], EDGE + 1, CAP)
    before = jnp.clip(counts[prv], EDGE + 1, CAP) - EDGE

    def place_slot(b, c):
        for o in range(27):
            name = nbr[b, o]
            owner = name >> 3
            inside = name & 7
            slot = jnp.where(
                owner == me, inside, jnp.where(owner < me, CAP + inside - before, CAP + EDGE + inside)
            )
            slots[b, o] = jnp.where(name < 0, ZERO, jnp.clip(slot, 0, ZERO))
        return c

    eye = (
        lax.broadcasted_iota(jnp.int32, (128, 128), 0)
        == lax.broadcasted_iota(jnp.int32, (128, 128), 1)
    ).astype(F32)
    ones = jnp.ones((128, 128), BF)

    def wide(rows):
        return jnp.dot((eye * rows).astype(BF), ones, preferred_element_type=F32)

    def widen(b, c):
        wv[b] = wide(mrow[b])
        return c

    def widen_edge(e, c):
        wv[CAP + e] = wide(me_row[e])
        return c

    for b in range(CAP):
        alive = jnp.where(live > b, 1.0, 0.0).astype(F32)
        mrow[b] = mask[b : b + 1, :].astype(F32) * alive
    lax.fori_loop(0, CAP, widen, 0)

    def weight(b):
        w = wv[b]
        return jnp.concatenate([w, w], axis=1)


    def fold(x):
        return jnp.sum(x.reshape(16, 8, 256), axis=0)

    def put_row(src, dst, send, recv_sem, target):
        pltpu.make_async_remote_copy(
            src_ref=src, dst_ref=dst, send_sem=send, recv_sem=recv_sem,
            device_id=target, device_id_type=MESH,
        ).start()

    def send_row(k, row):
        stat[k] = row
        recv[k, me] = row
        for other in others:
            put_row(stat.at[k], recv.at[k, me], ssem.at[k], rsem.at[k], other)

    def send_sub(k, row):
        first[k] = row
        rowa[k, sub] = row
        for t in range(1, ns):
            target = (region, lax.rem(sub + t, ns))
            put_row(first.at[k], rowa.at[k, sub], sas.at[k], sar.at[k], target)

    def send_region(k, combined):
        many(rowa, k, ns, sas, sar).wait_recv()
        row = combined(rowa[k])
        stat[k + 2] = row
        rowb[k, region] = row
        for t in range(1, nd // ns):
            target = (lax.rem(region + t, nd // ns), sub)
            put_row(stat.at[k + 2], rowb.at[k, region], sbs.at[k], sbr.at[k], target)

    def many(rows, k, size, send, recv_sem):
        block = rows.at[k, pl.ds(0, size - 1)]
        return pltpu.make_async_remote_copy(
            src_ref=block, dst_ref=block, send_sem=send.at[k], recv_sem=recv_sem.at[k],
            device_id=place(nxt), device_id_type=MESH,
        )

    def all_rows(k):
        return many(recv, k, nd, ssem, rsem)

    def exchange(k, ahead, back, edges, width):
        to_next = pltpu.make_async_remote_copy(
            src_ref=ahead, dst_ref=edges.at[0:width],
            send_sem=hs.at[2 * k], recv_sem=hr.at[2 * k], device_id=place(nxt), device_id_type=MESH,
        )
        to_prev = pltpu.make_async_remote_copy(
            src_ref=back, dst_ref=edges.at[width : 2 * width],
            send_sem=hs.at[2 * k + 1], recv_sem=hr.at[2 * k + 1], device_id=place(prv), device_id_type=MESH,
        )
        return to_next, to_prev

    def halo(k, staged, buffer, edges):
        return exchange(k, staged, buffer.at[0:EDGE], edges, EDGE)

    def stage(staged, buffer):
        for e in range(EDGE):
            staged[e] = buffer[live - EDGE + e]

    count_rows = lax.fori_loop(
        0, CAP, lambda b, a: a + jnp.sum(wv[b].reshape(16, 8, 128), axis=0), jnp.zeros((8, 128), F32)
    )
    local_n = jnp.sum(count_rows, axis=0, keepdims=True) * GC

    def local_sum(value):
        return lax.fori_loop(
            0, CAP, lambda b, a: a + fold(value(b) * weight(b)), jnp.zeros((8, 256), F32)
        )

    def local_stats(value, total):
        means = [s / jnp.maximum(local_n, 1.0) for s in group_total(total)]
        mean = jnp.concatenate(means, axis=1)

        def squares(b, a):
            d = value(b) - mean
            return a + fold(d * d * weight(b))

        m2 = group_total(lax.fori_loop(0, CAP, squares, jnp.zeros((8, 256), F32)))
        return pack_lanes({0: means[0], 1: m2[0], 2: means[1], 3: m2[1], 4: local_n, 6: local_n})

    def combine(rows):
        row = merge(rows)
        n = spread_lane(row, 4)
        mean = jnp.concatenate([spread_lane(row, 0), spread_lane(row, 2)], axis=1)
        spread = jnp.concatenate([spread_lane(row, 1) / n, spread_lane(row, 3) / n], axis=1)
        return mean, lax.rsqrt(spread + EPS), n

    def back_row(sums):
        first, second = group_total(sums[0]), group_total(sums[1])
        return pack_lanes({0: first[0], 1: second[0], 2: first[1], 3: second[1], 4: local_n})

    def back_means(row, n):
        first = jnp.concatenate([spread_lane(row, 0) / n, spread_lane(row, 2) / n], axis=1)
        second = jnp.concatenate([spread_lane(row, 1) / n, spread_lane(row, 3) / n], axis=1)
        return first, second

    def own_means(row):
        return back_means(row, jnp.maximum(spread_lane(row, 4), 1.0))

    def add_rows(rows):
        return jnp.sum(rows, axis=0)

    def put_variants(bank, s, a):
        a = a.reshape(16, 8, 256)
        for v, shift in enumerate((1, 0, 7)):
            q = (pltpu.roll(a, shift, 1) if shift else a).reshape(4, 4, 8, 256)
            bank[s, 2 * v] = q.reshape(4, 2, 16, 256).astype(BF)
            y = jnp.concatenate([q[:, 3:4], q[:, 0:3]], axis=1)
            bank[s, 2 * v + 1] = y.reshape(4, 2, 16, 256).astype(BF)

    row = lax.broadcasted_iota(jnp.int32, (16, 256), 0)
    z_first, z_last, upper = (row & 7) == 0, (row & 7) == 7, row < 8

    def gather(bank, b, to, at, v, i):
        xs = (slice(3, 4), slice(0, 4), slice(0, 1))[i]
        xd = (slice(0, 1), slice(1, 5), slice(5, 6))[i]

        def load(j, parity, pairs):
            here = bank[slots[b, i * 9 + j * 3 + 1], 2 * v + parity, xs, pairs]
            if v == 1:
                return here
            there = bank[slots[b, i * 9 + j * 3 + v], 2 * v + parity, xs, pairs]
            edge = jnp.broadcast_to(z_first if v == 0 else z_last, here.shape)
            return jnp.where(edge, there, here)

        to[at, v, xd, 0:2] = load(1, 0, slice(0, 2))
        wrap = load(1, 1, slice(0, 1))
        half = jnp.broadcast_to(upper, wrap.shape)
        to[at, v, xd, 2:3] = jnp.where(half, load(0, 1, slice(0, 1)), wrap)
        to[at, v, xd, 3:4] = load(1, 1, slice(1, 2))
        to[at, v, xd, 4:5] = jnp.where(half, wrap, load(2, 1, slice(0, 1)))

    def gather_brick(bank, to):
        def one(b, c):
            for v in range(3):
                for i in range(3):
                    gather(bank, b, to, b, v, i)
            return c

        return one

    def product(tiles, weights, back, pieces):
        acc, done = None, 0
        for o, (i, j, k) in enumerate(OFFSETS):
            left = tiles[:, k, i : i + 4, PAIR_START[j] : PAIR_START[j] + 2].reshape(HALF * 128, 256)
            if back:
                block = weights[(26 - o) * 256 : (27 - o) * 256, :]
                part = lax.dot_general(
                    left, block, (((1,), (1,)), ((), ())), preferred_element_type=F32
                )
            else:
                part = jnp.dot(
                    left, weights[o * 256 : (o + 1) * 256, :], preferred_element_type=F32
                )
            acc = part if acc is None else acc + part
            while done * 27 < len(pieces) * (o + 1):
                pieces[done]()
                done += 1
        return acc.reshape(HALF, 128, 256)

    def pieces_of(bank, first_brick, to):
        return [
            functools.partial(gather, bank, first_brick + b, to, b, v, i)
            for b in range(HALF) for v in range(3) for i in range(3)
        ]

    def first_tiles(bank):
        lax.fori_loop(0, HALF, gather_brick(bank, eo), 0)

    def conv(bank, weights, back, into, between=None, late=()):
        into[0:HALF] = product(eo, weights, back, pieces_of(bank, HALF, ep))
        if between is not None:
            between()
        into[HALF:CAP] = product(ep, weights, back, late)

    def each(body):
        return [functools.partial(body, b) for b in range(HALF)]

    gain1, bias1, gain2, bias2 = gain1_ref[...], bias1_ref[...], gain2_ref[...], bias2_ref[...]

    loads[0].wait()
    stage(sx, xb)
    stage(sm, mrow)

    def inputs(b):
        return xb[b].astype(F32) * weight(b)

    first_row = local_stats(inputs, local_sum(inputs))
    loads[1].wait()
    stage(sc, cb)

    def both(body, local, edge):
        lax.fori_loop(0, CAP, lambda b, c: body(b, *(r[b] for r in local)) or c, 0)
        lax.fori_loop(0, 2 * EDGE, lambda e, c: body(CAP + e, *(r[e] for r in edge)) or c, 0)

    def grad_branch(s, g):
        put_variants(sw, s, g.astype(F32) * weight(s))

    lax.fori_loop(0, CAP, place_slot, 0)

    for bank in (sv, sw):
        bank[ZERO] = jnp.zeros((6, 4, 2, 16, 256), BF)
    lax.fori_loop(0, CAP, lambda b, c: grad_branch(b, cb[b]) or c, 0)

    pl.semaphore_wait(barrier, nd - 1)

    mask_halo, feat_halo = halo(0, sm, mrow, me_row), halo(1, sx, xb, xe)
    cot_halo = halo(2, sc, cb, ce)
    send_row(0, first_row)
    for pair in (mask_halo, feat_halo, cot_halo):
        for c in pair:
            c.start()

    for c in mask_halo:
        c.wait_recv()
    lax.fori_loop(0, 2 * EDGE, widen_edge, 0)
    all_rows(0).wait_recv()
    mean1, inv1, n = combine(recv[0])

    def first_act(s, x):
        w = weight(s)
        normed = (x.astype(F32) * w - mean1) * inv1
        pre = normed * gain1 + bias1
        put_variants(sv, s, pre * jax.nn.sigmoid(pre) * w)

    lax.fori_loop(0, CAP, lambda b, c: first_act(b, xb[b]) or c, 0)
    for c in feat_halo:
        c.wait_recv()
    lax.fori_loop(0, 2 * EDGE, lambda e, c: first_act(CAP + e, xe[e]) or c, 0)
    loads[2].wait()

    zeros = jnp.zeros((8, 256), F32)
    accs[0] = zeros
    accs[1] = zeros

    def keep_hidden(b, c=0):
        w = weight(b)
        h = (fb[b] * w).astype(BF)
        hb[b] = h
        accs[0] += fold(h.astype(F32) * w)
        return c

    def cot_edges():
        for c in cot_halo:
            c.wait_recv()
        lax.fori_loop(0, 2 * EDGE, lambda e, c: grad_branch(CAP + e, ce[e]) or c, 0)

    first_tiles(sv)
    conv(sv, wt1, False, fb, late=each(keep_hidden))
    lax.fori_loop(HALF, CAP, keep_hidden, 0)
    stage(sh, hb)
    hidden_halo = halo(3, sh, hb, he)
    send_row(2, local_stats(lambda b: hb[b].astype(F32), accs[0]))
    for c in hidden_halo:
        c.start()

    cot_edges()
    loads[3].wait()
    first_tiles(sw)
    conv(sw, wt2, True, ga2)
    all_rows(2).wait_recv()
    mean2, inv2, _ = combine(recv[2])

    def slope_of(pre, s):
        return s * (1.0 + pre * (1.0 - s))

    def second_local(b, sums):
        w = weight(b)
        normed = (hb[b].astype(F32) - mean2) * inv2
        pre = normed * gain2 + bias2
        s = jax.nn.sigmoid(pre)
        put_variants(sv, b, pre * s * w)
        scaled = ga2[b] * slope_of(pre, s) * w * gain2
        sl[b] = scaled
        return sums[0] + fold(scaled), sums[1] + fold(scaled * normed)

    own_row = back_row(lax.fori_loop(0, CAP, second_local, (zeros, zeros)))
    send_sub(1, own_row)

    own_first, own_second = own_means(own_row)

    def residual(b):
        normed = (hb[b].astype(F32) - mean2) * inv2
        return (sl[b] - own_first - normed * own_second).astype(BF)

    for e in range(EDGE):
        rp[e] = residual(e)
        rn[e] = residual(live - EDGE + e)
    grad_halo = exchange(4, rn, rp, ge, EDGE)
    means_halo = exchange(5, first.at[pl.ds(1, 1)], first.at[pl.ds(1, 1)], nb, 1)
    for pair in (means_halo, grad_halo):
        for c in pair:
            c.start()

    for c in hidden_halo:
        c.wait_recv()

    def second_edge(e, c):
        s = CAP + e
        w = weight(s)
        pre = (he[e].astype(F32) - mean2) * inv2 * gain2 + bias2
        put_variants(sv, s, pre * jax.nn.sigmoid(pre) * w)
        return c

    lax.fori_loop(0, 2 * EDGE, second_edge, 0)

    def finish(b, c=0):
        w = weight(b)
        out[b] = ((xb[b].astype(F32) * w + fb[b]) * w).astype(BF)
        return c

    first_tiles(sv)
    conv(sv, wt2, False, fb, between=lambda: send_region(1, add_rows), late=each(finish))
    lax.fori_loop(HALF, CAP, finish, 0)

    many(rowb, 1, nd // ns, sbs, sbr).wait_recv()
    first2, second2 = back_means(add_rows(rowb[1]), n)

    def grad_hidden(s, h, scaled, along_first, along_second):
        normed = (h.astype(F32) - mean2) * inv2
        grad = inv2 * (scaled - along_first - normed * along_second) * weight(s)
        put_variants(sw, s, grad)

    lax.fori_loop(0, CAP, lambda b, c: grad_hidden(b, hb[b], sl[b], first2, second2) or c, 0)
    for pair in (means_halo, grad_halo):
        for c in pair:
            c.wait_recv()
    for side in range(2):
        side_first, side_second = own_means(nb[side])
        side_first, side_second = first2 - side_first, second2 - side_second

        def edge_grad(e, c):
            grad_hidden(CAP + e, he[e], ge[e].astype(F32), side_first, side_second)
            return c

        lax.fori_loop(side * EDGE, (side + 1) * EDGE, edge_grad, 0)

    accs[0] = zeros
    accs[1] = zeros

    def first_back(b, c=0):
        w = weight(b)
        normed = (xb[b].astype(F32) * w - mean1) * inv1
        pre = normed * gain1 + bias1
        scaled = fb[b] * slope_of(pre, jax.nn.sigmoid(pre)) * w * gain1
        sl[b] = scaled
        accs[0] += fold(scaled)
        accs[1] += fold(scaled * normed)
        return c

    first_tiles(sw)
    conv(sw, wt1, True, fb, late=each(first_back))
    lax.fori_loop(HALF, CAP, first_back, 0)
    send_row(1, back_row((accs[0], accs[1])))

    def before_means(b, c):
        normed = (xb[b].astype(F32) * weight(b) - mean1) * inv1
        sl[b] = cb[b].astype(F32) + inv1 * sl[b]
        fb[b] = inv1 * normed
        return c

    lax.fori_loop(0, CAP, before_means, 0)
    all_rows(1).wait_recv()
    first1, second1 = back_means(add_rows(recv[1]), n)
    first1 = inv1 * first1

    def grad_features(b, c):
        gfeat[b] = ((sl[b] - first1 - fb[b] * second1) * weight(b)).astype(BF)
        return c

    lax.fori_loop(0, CAP, grad_features, 0)

    for k in range(3):
        all_rows(k).wait_send()
    many(rowa, 1, ns, sas, sar).wait_send()
    many(rowb, 1, nd // ns, sbs, sbr).wait_send()
    for pair in (mask_halo, feat_halo, cot_halo, hidden_halo, grad_halo, means_halo):
        for c in pair:
            c.wait_send()


def solution(mesh):
    ns = mesh.shape["sub"]
    nd = mesh.shape["region"] * ns

    def on_device(
        features, voxel_mask, counts, neighbors, w_first, w_second,
        gain_first, bias_first, gain_second, bias_second, cotangent,
    ):
        gains = [v.reshape(1, 256) for v in (gain_first, bias_first, gain_second, bias_second)]
        vmem = pl.BlockSpec(memory_space=pltpu.VMEM)
        smem = pl.BlockSpec(memory_space=pltpu.SMEM)
        hbm = pl.BlockSpec(memory_space=pl.ANY)
        shape = features.shape
        dma = pltpu.SemaphoreType.DMA
        results = pl.pallas_call(
            functools.partial(kernel, nd, ns),
            out_shape=(pltpu.VMEM(shape, BF), pltpu.VMEM(shape, BF)),
            in_specs=[hbm, vmem, smem, smem, hbm, hbm, vmem, vmem, vmem, vmem, hbm],
            out_specs=(vmem, vmem),
            scratch_shapes=[
                pltpu.VMEM((CAP, 128, 256), BF),
                pltpu.VMEM((CAP, 128, 256), BF),
                pltpu.VMEM((CAP, 128, 256), BF),
                pltpu.VMEM((CAP, 128, 256), F32),
                pltpu.VMEM((2 * EDGE, 128, 256), BF),
                pltpu.VMEM((2 * EDGE, 128, 256), BF),
                pltpu.VMEM((2 * EDGE, 128, 256), BF),
                pltpu.VMEM((2 * EDGE, 128, 256), BF),
                pltpu.VMEM((CAP, 128, 256), F32),
                pltpu.VMEM((CAP, 128, 256), F32),
                pltpu.VMEM((CAP, 1, 128), F32),
                pltpu.VMEM((2 * EDGE, 1, 128), F32),
                pltpu.VMEM((EXT, 128, 128), F32),
                pltpu.VMEM((EXT + 1, 6, 4, 2, 16, 256), BF),
                pltpu.VMEM((EXT + 1, 6, 4, 2, 16, 256), BF),
                pltpu.VMEM((HALF, 3, 6, 5, 16, 256), BF),
                pltpu.VMEM((HALF, 3, 6, 5, 16, 256), BF),
                pltpu.VMEM((6912, 256), BF),
                pltpu.VMEM((6912, 256), BF),
                pltpu.VMEM((EDGE, 128, 256), BF),
                pltpu.VMEM((EDGE, 128, 256), BF),
                pltpu.VMEM((EDGE, 128, 256), BF),
                pltpu.VMEM((EDGE, 128, 256), BF),
                pltpu.VMEM((EDGE, 128, 256), BF),
                pltpu.VMEM((EDGE, 1, 128), F32),
                pltpu.VMEM((2, 1, 128), F32),
                pltpu.VMEM((2, 8, 256), F32),
                pltpu.VMEM((4, 1, 128), F32),
                pltpu.VMEM((2, 1, 128), F32),
                pltpu.VMEM((3, nd, 1, 128), F32),
                pltpu.VMEM((2, ns, 1, 128), F32),
                pltpu.VMEM((2, nd // ns, 1, 128), F32),
                pltpu.SMEM((CAP, 27), jnp.int32),
                dma((4,)),
                dma((3,)),
                dma((3,)),
                dma((2,)),
                dma((2,)),
                dma((2,)),
                dma((2,)),
                dma((12,)),
                dma((12,)),
            ],
            compiler_params=pltpu.CompilerParams(
                collective_id=0, has_side_effects=True, vmem_limit_bytes=56 * 2**20
            ),
        )(features, voxel_mask, counts, neighbors, w_first, w_second, *gains, cotangent)
        return tuple(results)

    bricks = P(("region", "sub"), None, None)
    rows = P(("region", "sub"), None)
    return jax.shard_map(
        on_device,
        mesh=mesh,
        in_specs=(bricks, rows, P(), rows, P(), P(), P(), P(), P(), P(), bricks),
        out_specs=(bricks, bricks),
        check_vma=False,
    )
```

```python
import functools

import jax
import jax.numpy as jnp
from jax import lax
from jax.experimental import pallas as pl
from jax.experimental.pallas import tpu as pltpu
from jax.sharding import PartitionSpec as P

GC = 8
CAP = 8
EDGE = 3
EXT = CAP + 2 * EDGE
ZERO = EXT
EPS = 1e-05
HALF = CAP // 2
MESH = pl.DeviceIdType.MESH
BF = jnp.bfloat16
F32 = jnp.float32
OFFSETS = [(i, j, k) for i in range(3) for j in range(3) for k in range(3)]
PAIR_START = (2, 0, 3)


def hops(step, size):
    return min(step % size, -step % size)


def far_first(nd):
    steps = [(x, c, y, z) for x in range(4) for c in range(2) for y in range(4) for z in range(4)]
    return sorted(steps[1:], key=lambda s: -hops(s[0], 4) - hops(s[2], 4) - hops(s[3], 4))


def lane_bits(shape):
    return lax.broadcasted_iota(jnp.int32, shape, len(shape) - 1) & 7


def group_sum(x):
    lane = lax.broadcasted_iota(jnp.int32, x.shape, 1)
    for step in (1, 2, 4):
        up = pltpu.roll(x, 128 - step, 1)
        down = pltpu.roll(x, step, 1)
        x = x + jnp.where((lane & step) == 0, up, down)
    return x


def group_total(x):
    return [
        jnp.sum(group_sum(x[:, h * 128 : (h + 1) * 128]), axis=0, keepdims=True) for h in range(2)
    ]


def spread_lane(row, lane):
    wide = jnp.broadcast_to(row, (8, 128))
    return group_sum(jnp.where(lane_bits((8, 128)) == lane, wide, 0.0))[0:1]


def loop(lo, hi, body, init):
    width = next(u for u in range(2, 0, -1) if (hi - lo) % u == 0)

    def trip(t, c):
        for u in range(width):
            c = body(lo + t * width + u, c)
        return c

    return lax.fori_loop(0, (hi - lo) // width, trip, init)


def roll_row(row, step):
    return pltpu.roll(jnp.broadcast_to(row, (8, 128)), step, 1)[0:1]


def merge(rows):
    total = jnp.sum(rows, axis=0)
    counts = pltpu.roll(rows, 124, 2)
    weighted = jnp.sum(rows * counts, axis=0)
    n = roll_row(total, 124)
    bits = lane_bits((1, 128))
    is_mean = (bits == 0) | (bits == 2)
    mean = jnp.where(is_mean, weighted / jnp.maximum(n, 1.0), 0.0)
    d = rows - mean
    between = jnp.where(is_mean, jnp.sum(d * d * counts, axis=0), 0.0)
    return jnp.where(is_mean, mean, total + roll_row(between, 1))


def pack_lanes(parts):
    bits = lane_bits((1, 128))
    row = jnp.zeros((1, 128), F32)
    for c, part in parts.items():
        row = jnp.where(bits == c, part, row)
    return row


def kernel(
    nd, ns,
    feat, mask, counts, nbr, w1, w2, gain1_ref, bias1_ref, gain2_ref, bias2_ref, cot,
    out, gfeat,
    xb, cb, hb, ga2, xe, ce, he, ge, fb, sl, mrow, me_row, wv, sv, sw, eo, ep, wt1, wt2,
    sx, sc, sh, rn, rp, sm, nb, accs, stat, first, recv, rowa, rowb, slots,
    lsem, ssem, rsem, sas, sar, sbs, sbr, hs, hr,
):
    region, sub = lax.axis_index("region"), lax.axis_index("sub")
    me = region * ns + sub
    nxt, prv = lax.rem(me + 1, nd), lax.rem(me + nd - 1, nd)

    def place(o):
        return (lax.div(o, ns), lax.rem(o, ns))

    loads = [
        pltpu.make_async_copy(feat, xb, lsem.at[0]),
        pltpu.make_async_copy(cot, cb, lsem.at[1]),
        pltpu.make_async_copy(w1, wt1, lsem.at[2]),
        pltpu.make_async_copy(w2, wt2, lsem.at[3]),
    ]
    for c in loads:
        c.start()

    barrier = pltpu.get_barrier_semaphore()

    if nd == 128:
        xs = [lax.rem(lax.div(region, 2) + t, 4) * 2 for t in range(4)]
        cs = [lax.rem(region + t, 2) for t in range(2)]
        ys = [lax.rem(lax.div(sub, 4) + t, 4) * 4 for t in range(4)]
        zs = [lax.rem(sub + t, 4) for t in range(4)]
        others = [(xs[x] + cs[c], ys[y] + zs[z]) for x, c, y, z in far_first(nd)]
    else:
        others = [place(lax.rem(me + t, nd)) for t in range(1, nd)]
    for other in others:
        pl.semaphore_signal(barrier, inc=1, device_id=other, device_id_type=MESH)

    live = jnp.clip(counts[me], EDGE + 1, CAP)
    before = jnp.clip(counts[prv], EDGE + 1, CAP) - EDGE

    def place_slot(b, c):
        for o in range(27):
            name = nbr[b, o]
            owner = name >> 3
            inside = name & 7
            slot = jnp.where(
                owner == me, inside, jnp.where(owner < me, CAP + inside - before, CAP + EDGE + inside)
            )
            slots[b, o] = jnp.where(name < 0, ZERO, jnp.clip(slot, 0, ZERO))
        return c

    eye = (
        lax.broadcasted_iota(jnp.int32, (128, 128), 0)
        == lax.broadcasted_iota(jnp.int32, (128, 128), 1)
    ).astype(F32)
    ones = jnp.ones((128, 128), BF)

    def wide(rows):
        return jnp.dot((eye * rows).astype(BF), ones, preferred_element_type=F32)

    def widen(b, c):
        wv[b] = wide(mrow[b])
        return c

    def widen_edge(e, c):
        wv[CAP + e] = wide(me_row[e])
        return c

    for b in range(CAP):
        alive = jnp.where(live > b, 1.0, 0.0).astype(F32)
        mrow[b] = mask[b : b + 1, :].astype(F32) * alive
    loop(0, CAP, widen, 0)

    def weight(b):
        w = wv[b]
        return jnp.concatenate([w, w], axis=1)


    def fold(x):
        return jnp.sum(x.reshape(16, 8, 256), axis=0)

    def put_row(src, dst, send, recv_sem, target):
        pltpu.make_async_remote_copy(
            src_ref=src, dst_ref=dst, send_sem=send, recv_sem=recv_sem,
            device_id=target, device_id_type=MESH,
        ).start()

    def send_row(k, row):
        stat[k] = row
        recv[k, me] = row
        for other in others:
            put_row(stat.at[k], recv.at[k, me], ssem.at[k], rsem.at[k], other)

    def send_sub(k, row):
        first[k] = row
        rowa[k, sub] = row
        for t in range(1, ns):
            target = (region, lax.rem(sub + t, ns))
            put_row(first.at[k], rowa.at[k, sub], sas.at[k], sar.at[k], target)

    def send_region(k, combined):
        many(rowa, k, ns, sas, sar).wait_recv()
        row = combined(rowa[k])
        stat[k + 2] = row
        rowb[k, region] = row
        for t in range(1, nd // ns):
            target = (lax.rem(region + t, nd // ns), sub)
            put_row(stat.at[k + 2], rowb.at[k, region], sbs.at[k], sbr.at[k], target)

    def many(rows, k, size, send, recv_sem):
        block = rows.at[k, pl.ds(0, size - 1)]
        return pltpu.make_async_remote_copy(
            src_ref=block, dst_ref=block, send_sem=send.at[k], recv_sem=recv_sem.at[k],
            device_id=place(nxt), device_id_type=MESH,
        )

    def all_rows(k):
        return many(recv, k, nd, ssem, rsem)

    def exchange(k, ahead, back, edges, width):
        to_next = pltpu.make_async_remote_copy(
            src_ref=ahead, dst_ref=edges.at[0:width],
            send_sem=hs.at[2 * k], recv_sem=hr.at[2 * k], device_id=place(nxt), device_id_type=MESH,
        )
        to_prev = pltpu.make_async_remote_copy(
            src_ref=back, dst_ref=edges.at[width : 2 * width],
            send_sem=hs.at[2 * k + 1], recv_sem=hr.at[2 * k + 1], device_id=place(prv), device_id_type=MESH,
        )
        return to_next, to_prev

    def halo(k, staged, buffer, edges):
        return exchange(k, staged, buffer.at[0:EDGE], edges, EDGE)

    def stage(staged, buffer):
        for e in range(EDGE):
            staged[e] = buffer[live - EDGE + e]

    count_rows = loop(
        0, CAP, lambda b, a: a + jnp.sum(wv[b].reshape(16, 8, 128), axis=0), jnp.zeros((8, 128), F32)
    )
    local_n = jnp.sum(count_rows, axis=0, keepdims=True) * GC

    def local_sum(value):
        return loop(
            0, CAP, lambda b, a: a + fold(value(b) * weight(b)), jnp.zeros((8, 256), F32)
        )

    def local_stats(value, total):
        means = [s / jnp.maximum(local_n, 1.0) for s in group_total(total)]
        mean = jnp.concatenate(means, axis=1)

        def squares(b, a):
            d = value(b) - mean
            return a + fold(d * d * weight(b))

        m2 = group_total(loop(0, CAP, squares, jnp.zeros((8, 256), F32)))
        return pack_lanes({0: means[0], 1: m2[0], 2: means[1], 3: m2[1], 4: local_n, 6: local_n})

    def combine(rows):
        row = merge(rows)
        n = spread_lane(row, 4)
        mean = jnp.concatenate([spread_lane(row, 0), spread_lane(row, 2)], axis=1)
        spread = jnp.concatenate([spread_lane(row, 1) / n, spread_lane(row, 3) / n], axis=1)
        return mean, lax.rsqrt(spread + EPS), n

    def back_row(sums):
        first, second = group_total(sums[0]), group_total(sums[1])
        return pack_lanes({0: first[0], 1: second[0], 2: first[1], 3: second[1], 4: local_n})

    def back_means(row, n):
        first = jnp.concatenate([spread_lane(row, 0) / n, spread_lane(row, 2) / n], axis=1)
        second = jnp.concatenate([spread_lane(row, 1) / n, spread_lane(row, 3) / n], axis=1)
        return first, second

    def own_means(row):
        return back_means(row, jnp.maximum(spread_lane(row, 4), 1.0))

    def add_rows(rows):
        return jnp.sum(rows, axis=0)

    def put_variants(bank, s, a):
        a = a.reshape(16, 8, 256)
        for v, shift in enumerate((1, 0, 7)):
            q = (pltpu.roll(a, shift, 1) if shift else a).reshape(4, 4, 8, 256)
            bank[s, 2 * v] = q.reshape(4, 2, 16, 256).astype(BF)
            y = jnp.concatenate([q[:, 3:4], q[:, 0:3]], axis=1)
            bank[s, 2 * v + 1] = y.reshape(4, 2, 16, 256).astype(BF)

    row = lax.broadcasted_iota(jnp.int32, (16, 256), 0)
    z_first, z_last, upper = (row & 7) == 0, (row & 7) == 7, row < 8

    def gather(bank, b, to, at, v, i):
        xs = (slice(3, 4), slice(0, 4), slice(0, 1))[i]
        xd = (slice(0, 1), slice(1, 5), slice(5, 6))[i]

        def load(j, parity, pairs):
            here = bank[slots[b, i * 9 + j * 3 + 1], 2 * v + parity, xs, pairs]
            if v == 1:
                return here
            there = bank[slots[b, i * 9 + j * 3 + v], 2 * v + parity, xs, pairs]
            edge = jnp.broadcast_to(z_first if v == 0 else z_last, here.shape)
            return jnp.where(edge, there, here)

        to[at, v, xd, 0:2] = load(1, 0, slice(0, 2))
        wrap = load(1, 1, slice(0, 1))
        half = jnp.broadcast_to(upper, wrap.shape)
        to[at, v, xd, 2:3] = jnp.where(half, load(0, 1, slice(0, 1)), wrap)
        to[at, v, xd, 3:4] = load(1, 1, slice(1, 2))
        to[at, v, xd, 4:5] = jnp.where(half, wrap, load(2, 1, slice(0, 1)))

    def gather_brick(bank, to):
        def one(b, c):
            for v in range(3):
                for i in range(3):
                    gather(bank, b, to, b, v, i)
            return c

        return one

    def product(tiles, weights, back, pieces):
        acc, done = None, 0
        for o, (i, j, k) in enumerate(OFFSETS):
            left = tiles[:, k, i : i + 4, PAIR_START[j] : PAIR_START[j] + 2].reshape(HALF * 128, 256)
            if back:
                block = weights[(26 - o) * 256 : (27 - o) * 256, :]
                part = lax.dot_general(
                    left, block, (((1,), (1,)), ((), ())), preferred_element_type=F32
                )
            else:
                part = jnp.dot(
                    left, weights[o * 256 : (o + 1) * 256, :], preferred_element_type=F32
                )
            acc = part if acc is None else acc + part
            while done * 27 < len(pieces) * (o + 1):
                pieces[done]()
                done += 1
        return acc.reshape(HALF, 128, 256)

    def pieces_of(bank, first_brick, to):
        return [
            functools.partial(gather, bank, first_brick + b, to, b, v, i)
            for b in range(HALF) for v in range(3) for i in range(3)
        ]

    def first_tiles(bank):
        loop(0, HALF, gather_brick(bank, eo), 0)

    def conv(bank, weights, back, into, between=None, late=()):
        into[0:HALF] = product(eo, weights, back, pieces_of(bank, HALF, ep))
        if between is not None:
            between()
        into[HALF:CAP] = product(ep, weights, back, late)

    def each(body):
        return [functools.partial(body, b) for b in range(HALF)]

    gain1, bias1, gain2, bias2 = gain1_ref[...], bias1_ref[...], gain2_ref[...], bias2_ref[...]

    loads[0].wait()
    stage(sx, xb)
    stage(sm, mrow)

    def inputs(b):
        return xb[b].astype(F32) * weight(b)

    first_row = local_stats(inputs, local_sum(inputs))
    loads[1].wait()
    stage(sc, cb)

    def both(body, local, edge):
        loop(0, CAP, lambda b, c: body(b, *(r[b] for r in local)) or c, 0)
        loop(0, 2 * EDGE, lambda e, c: body(CAP + e, *(r[e] for r in edge)) or c, 0)

    def grad_branch(s, g):
        put_variants(sw, s, g.astype(F32) * weight(s))

    lax.fori_loop(0, CAP, place_slot, 0)

    for bank in (sv, sw):
        bank[ZERO] = jnp.zeros((6, 4, 2, 16, 256), BF)
    loop(0, CAP, lambda b, c: grad_branch(b, cb[b]) or c, 0)

    pl.semaphore_wait(barrier, nd - 1)

    mask_halo, feat_halo = halo(0, sm, mrow, me_row), halo(1, sx, xb, xe)
    cot_halo = halo(2, sc, cb, ce)
    send_row(0, first_row)
    for pair in (mask_halo, feat_halo, cot_halo):
        for c in pair:
            c.start()

    for c in mask_halo:
        c.wait_recv()
    loop(0, 2 * EDGE, widen_edge, 0)
    all_rows(0).wait_recv()
    mean1, inv1, n = combine(recv[0])

    def first_act(s, x):
        w = weight(s)
        normed = (x.astype(F32) * w - mean1) * inv1
        pre = normed * gain1 + bias1
        put_variants(sv, s, pre * jax.nn.sigmoid(pre) * w)

    loop(0, CAP, lambda b, c: first_act(b, xb[b]) or c, 0)
    for c in feat_halo:
        c.wait_recv()
    loop(0, 2 * EDGE, lambda e, c: first_act(CAP + e, xe[e]) or c, 0)
    loads[2].wait()

    zeros = jnp.zeros((8, 256), F32)
    accs[0] = zeros
    accs[1] = zeros

    def keep_hidden(b, c=0):
        w = weight(b)
        h = (fb[b] * w).astype(BF)
        hb[b] = h
        accs[0] += fold(h.astype(F32) * w)
        return c

    def cot_edges():
        for c in cot_halo:
            c.wait_recv()
        loop(0, 2 * EDGE, lambda e, c: grad_branch(CAP + e, ce[e]) or c, 0)

    first_tiles(sv)
    conv(sv, wt1, False, fb, late=each(keep_hidden))
    loop(HALF, CAP, keep_hidden, 0)
    stage(sh, hb)
    hidden_halo = halo(3, sh, hb, he)
    send_row(2, local_stats(lambda b: hb[b].astype(F32), accs[0]))
    for c in hidden_halo:
        c.start()

    cot_edges()
    loads[3].wait()
    first_tiles(sw)
    conv(sw, wt2, True, ga2)
    all_rows(2).wait_recv()
    mean2, inv2, _ = combine(recv[2])

    def slope_of(pre, s):
        return s * (1.0 + pre * (1.0 - s))

    def second_local(b, sums):
        w = weight(b)
        normed = (hb[b].astype(F32) - mean2) * inv2
        pre = normed * gain2 + bias2
        s = jax.nn.sigmoid(pre)
        put_variants(sv, b, pre * s * w)
        scaled = ga2[b] * slope_of(pre, s) * w * gain2
        sl[b] = scaled
        return sums[0] + fold(scaled), sums[1] + fold(scaled * normed)

    own_row = back_row(loop(0, CAP, second_local, (zeros, zeros)))
    send_row(3, own_row)

    own_first, own_second = own_means(own_row)

    def residual(b):
        normed = (hb[b].astype(F32) - mean2) * inv2
        return (sl[b] - own_first - normed * own_second).astype(BF)

    for e in range(EDGE):
        rp[e] = residual(e)
        rn[e] = residual(live - EDGE + e)
    grad_halo = exchange(4, rn, rp, ge, EDGE)
    means_halo = exchange(5, stat.at[pl.ds(3, 1)], stat.at[pl.ds(3, 1)], nb, 1)
    for pair in (means_halo, grad_halo):
        for c in pair:
            c.start()

    for c in hidden_halo:
        c.wait_recv()

    def second_edge(e, c):
        s = CAP + e
        w = weight(s)
        pre = (he[e].astype(F32) - mean2) * inv2 * gain2 + bias2
        put_variants(sv, s, pre * jax.nn.sigmoid(pre) * w)
        return c

    loop(0, 2 * EDGE, second_edge, 0)

    def finish(b, c=0):
        w = weight(b)
        out[b] = ((xb[b].astype(F32) * w + fb[b]) * w).astype(BF)
        return c

    first_tiles(sv)
    conv(sv, wt2, False, fb, late=each(finish))
    loop(HALF, CAP, finish, 0)

    all_rows(3).wait_recv()
    first2, second2 = back_means(add_rows(recv[3]), n)

    def grad_hidden(s, h, scaled, along_first, along_second):
        normed = (h.astype(F32) - mean2) * inv2
        grad = inv2 * (scaled - along_first - normed * along_second) * weight(s)
        put_variants(sw, s, grad)

    loop(0, CAP, lambda b, c: grad_hidden(b, hb[b], sl[b], first2, second2) or c, 0)
    for pair in (means_halo, grad_halo):
        for c in pair:
            c.wait_recv()
    for side in range(2):
        side_first, side_second = own_means(nb[side])
        side_first, side_second = first2 - side_first, second2 - side_second

        def edge_grad(e, c):
            grad_hidden(CAP + e, he[e], ge[e].astype(F32), side_first, side_second)
            return c

        loop(side * EDGE, (side + 1) * EDGE, edge_grad, 0)

    accs[0] = zeros
    accs[1] = zeros

    def first_back(b, c=0):
        w = weight(b)
        normed = (xb[b].astype(F32) * w - mean1) * inv1
        pre = normed * gain1 + bias1
        scaled = fb[b] * slope_of(pre, jax.nn.sigmoid(pre)) * w * gain1
        sl[b] = scaled
        accs[0] += fold(scaled)
        accs[1] += fold(scaled * normed)
        return c

    first_tiles(sw)
    conv(sw, wt1, True, fb, late=each(first_back))
    loop(HALF, CAP, first_back, 0)
    send_row(1, back_row((accs[0], accs[1])))

    def before_means(b, c):
        normed = (xb[b].astype(F32) * weight(b) - mean1) * inv1
        sl[b] = cb[b].astype(F32) + inv1 * sl[b]
        fb[b] = inv1 * normed
        return c

    loop(0, CAP, before_means, 0)
    all_rows(1).wait_recv()
    first1, second1 = back_means(add_rows(recv[1]), n)
    first1 = inv1 * first1

    def grad_features(b, c):
        gfeat[b] = ((sl[b] - first1 - fb[b] * second1) * weight(b)).astype(BF)
        return c

    loop(0, CAP, grad_features, 0)

    for k in range(4):
        all_rows(k).wait_send()
    for pair in (mask_halo, feat_halo, cot_halo, hidden_halo, grad_halo, means_halo):
        for c in pair:
            c.wait_send()


def solution(mesh):
    ns = mesh.shape["sub"]
    nd = mesh.shape["region"] * ns

    def on_device(
        features, voxel_mask, counts, neighbors, w_first, w_second,
        gain_first, bias_first, gain_second, bias_second, cotangent,
    ):
        gains = [v.reshape(1, 256) for v in (gain_first, bias_first, gain_second, bias_second)]
        vmem = pl.BlockSpec(memory_space=pltpu.VMEM)
        smem = pl.BlockSpec(memory_space=pltpu.SMEM)
        hbm = pl.BlockSpec(memory_space=pl.ANY)
        shape = features.shape
        dma = pltpu.SemaphoreType.DMA
        results = pl.pallas_call(
            functools.partial(kernel, nd, ns),
            out_shape=(pltpu.VMEM(shape, BF), pltpu.VMEM(shape, BF)),
            in_specs=[hbm, vmem, smem, smem, hbm, hbm, vmem, vmem, vmem, vmem, hbm],
            out_specs=(vmem, vmem),
            scratch_shapes=[
                pltpu.VMEM((CAP, 128, 256), BF),
                pltpu.VMEM((CAP, 128, 256), BF),
                pltpu.VMEM((CAP, 128, 256), BF),
                pltpu.VMEM((CAP, 128, 256), F32),
                pltpu.VMEM((2 * EDGE, 128, 256), BF),
                pltpu.VMEM((2 * EDGE, 128, 256), BF),
                pltpu.VMEM((2 * EDGE, 128, 256), BF),
                pltpu.VMEM((2 * EDGE, 128, 256), BF),
                pltpu.VMEM((CAP, 128, 256), F32),
                pltpu.VMEM((CAP, 128, 256), F32),
                pltpu.VMEM((CAP, 1, 128), F32),
                pltpu.VMEM((2 * EDGE, 1, 128), F32),
                pltpu.VMEM((EXT, 128, 128), F32),
                pltpu.VMEM((EXT + 1, 6, 4, 2, 16, 256), BF),
                pltpu.VMEM((EXT + 1, 6, 4, 2, 16, 256), BF),
                pltpu.VMEM((HALF, 3, 6, 5, 16, 256), BF),
                pltpu.VMEM((HALF, 3, 6, 5, 16, 256), BF),
                pltpu.VMEM((6912, 256), BF),
                pltpu.VMEM((6912, 256), BF),
                pltpu.VMEM((EDGE, 128, 256), BF),
                pltpu.VMEM((EDGE, 128, 256), BF),
                pltpu.VMEM((EDGE, 128, 256), BF),
                pltpu.VMEM((EDGE, 128, 256), BF),
                pltpu.VMEM((EDGE, 128, 256), BF),
                pltpu.VMEM((EDGE, 1, 128), F32),
                pltpu.VMEM((2, 1, 128), F32),
                pltpu.VMEM((2, 8, 256), F32),
                pltpu.VMEM((4, 1, 128), F32),
                pltpu.VMEM((2, 1, 128), F32),
                pltpu.VMEM((4, nd, 1, 128), F32),
                pltpu.VMEM((2, ns, 1, 128), F32),
                pltpu.VMEM((2, nd // ns, 1, 128), F32),
                pltpu.SMEM((CAP, 27), jnp.int32),
                dma((4,)),
                dma((4,)),
                dma((4,)),
                dma((2,)),
                dma((2,)),
                dma((2,)),
                dma((2,)),
                dma((12,)),
                dma((12,)),
            ],
            compiler_params=pltpu.CompilerParams(
                collective_id=0, has_side_effects=True, vmem_limit_bytes=56 * 2**20
            ),
        )(features, voxel_mask, counts, neighbors, w_first, w_second, *gains, cotangent)
        return tuple(results)

    bricks = P(("region", "sub"), None, None)
    rows = P(("region", "sub"), None)
    return jax.shard_map(
        on_device,
        mesh=mesh,
        in_specs=(bricks, rows, P(), rows, P(), P(), P(), P(), P(), P(), bricks),
        out_specs=(bricks, bricks),
        check_vma=False,
    )
```
